512 devices in a mesh: gz: 8 (over x, core), gy: 8 (over z), gx: 8 (over y).
Axes of the slice: x: 4, y: 8, z: 8, core: 2. Of those that a mesh axis runs over, the one named last changes fastest.
Arguments:
- source: float32 [2, 64, 256, 1024], P(None, 'gz', 'gy', 'gx'), may hold values from -6 to 6
- adjoint_start: float32 [2, 64, 256, 1024], P(None, 'gz', 'gy', 'gx'), may hold values from -4 to 4
- couple: float32 [6, 64, 256, 1024], P(None, 'gz', 'gy', 'gx'), may hold values from 0.15 to 2.4
- diag_inverse: float32 [2, 64, 256, 1024], P(None, 'gz', 'gy', 'gx'), may hold values from 0.1 to 0.16
- cross_inverse: float32 [2, 64, 256, 1024], P(None, 'gz', 'gy', 'gx'), may hold values from -0.04 to 0.04
- perf_row: int32 [8, 8, 8, 64], P('gz', 'gy', 'gx'), may hold values from 0 to 255, as said below
- well_owner: int32 [8, 8, 8, 64, 1], P('gz', 'gy', 'gx'), may hold values from 0 to 63; in each aligned block of 64 rows (0 to 63, 64 to 127, ..., all dimensions but the last counted through in order) at most 2 rows name the same one
- well_slot: int32 [8, 8, 8, 64], P('gz', 'gy', 'gx'), may hold values from 0 to 3
- well_block: bfloat16 [8, 8, 8, 4, 256, 256], P('gz', 'gy', 'gx'), may hold values from -0.375 to 0.375
- cross_block: bfloat16 [8, 8, 8, 4, 256, 256], P('gz', 'gy', 'gx'), may hold values from -0.09375 to 0.09375
Outputs:
- adjoint: float32 [2, 64, 256, 1024], P(None, 'gz', 'gy', 'gx')
The draws below stay inside these ranges and needn't reach their ends.
Inputs may be any that keep to these rules, and one draw needn't show every extreme that they name: `perf_row`: the 64 rows of one device are distinct. `well_owner`: at most 2 of one device's panels name the same owner.
All inputs are finite; a program needn't handle non-finite values.
Results may differ from the reference program's by a relative error of at most 0.0015.
Values may be sent and summed in bfloat16 or wider, within the bound.
No kernel may reach another device: no remote copies, remote signals or barrier semaphores. Data moves between devices by JAX's collectives and lax.ppermute only.
A program may use at most 64 MiB of HBM per device.

```python
import math
import jax
import jax.numpy as jnp
import numpy as np
from jax import lax

CX = 128
CY = 32
CZ = 8
PANELS = 64
WELL_DEV = 4
SWEEPS = 4
OUTER = 2
ZDEVS = 8
YDEVS = 8
XDEVS = 8
NZ = 64
NY = 256
NX = 1024
CAP = 2


def draw_perf_row(key, part):
    device_count = ZDEVS * YDEVS * XDEVS
    device_keys = jax.random.split(jax.random.fold_in(key, 17), device_count)

    def one_device(device_key):
        return jax.random.permutation(device_key, CZ * CY)[:PANELS]
    picked_rows = jax.vmap(one_device)(device_keys)
    return picked_rows.reshape(ZDEVS, YDEVS, XDEVS, PANELS).astype(jnp.int32)


def set_ends(entries, stream_key, low, largest):
    index_at = [jax.random.randint(jax.random.fold_in(stream_key, axis), (), 0, length) for axis, length in enumerate(entries.shape)]
    longest = entries.shape.index(max(entries.shape))
    next_to = index_at[:longest] + [(index_at[longest] + 1) % entries.shape[longest]] + index_at[longest + 1:]
    return entries.at[tuple(index_at)].set(low).at[tuple(next_to)].set(largest)


def block_levels(key, shape, cuts, smallest, largest):
    def one(dim, shards_of):
        draws = jax.random.uniform(jax.random.fold_in(jax.random.fold_in(key, 6), dim), (shards_of,), jnp.float32, smallest / len(cuts), largest / len(cuts))
        return jnp.repeat(jnp.exp(draws), shape[dim] // shards_of).reshape((-1,) + (1,) * (len(shape) - dim - 1))

    level = one(*cuts[0])
    for cut in cuts[1:]:
        level = level * one(*cut)
    return level


def assign_block(rng, own, number, rows, number_of, top, bound, skew):
    sequence = jax.random.permutation(rng, number_of)
    heavy_load, common = shares(number_of, rows * top, bound, skew, True), shares(number_of, rows * top, bound, skew, False)
    places = jnp.arange(number_of)

    def named(sizes, turn):
        used = int((sizes > 0).sum())
        fixed = max(1, used // 4)
        passed = fixed + (places - fixed + turn * (used - fixed)) % max(1, number_of - fixed)
        return jnp.zeros((number_of,), jnp.int32).at[sequence[jnp.where(places < fixed, places, passed)]].set(jnp.asarray(sizes, jnp.int32))

    sizes = jnp.where(number % 4 == 0, named(heavy_load, number // 4), named(common, number - number // 4 - 1))
    mixed = jax.random.permutation(jax.random.fold_in(own, 3), number_of)
    giver, taker = mixed[0:number_of // 2 * 2:2], mixed[1:number_of // 2 * 2:2]
    margin = jnp.minimum(sizes[giver] - 1, bound - sizes[taker]) // 2
    margin = jnp.where((giver == sequence[0]) | (taker == sequence[0]) | (sizes[taker] == 0), 0, jnp.maximum(margin, 0))
    passed = jax.random.randint(jax.random.fold_in(own, 4), (number_of // 2,), 0, 1 << 20) % (margin + 1)
    sizes = sizes.at[giver].add(-passed).at[taker].add(passed)
    members = jnp.searchsorted(jnp.cumsum(sizes), jnp.arange(rows * top), side="right").astype(jnp.int32)
    table = members.reshape(top, rows).T
    table = table[jax.random.permutation(jax.random.fold_in(own, 1), rows)]
    turn = jax.random.randint(jax.random.fold_in(own, 2), (rows, 1), 0, top)
    return jnp.take_along_axis(table, (jnp.arange(top)[None, :] + turn) % top, axis=1)


def shares(count, total, most, lean, full):
    loads = [(1 << 20) // math.isqrt(rank ** lean) + 1 for rank in range(1, count + 1)]
    largest = most if full else min(most, max(-(-total // count), total * loads[0] // sum(loads)))
    least = 1 if total - largest >= count - 1 else 0
    given, surplus = [largest] + [least] * (count - 1), total - largest - least * (count - 1)
    while surplus > 0:
        candidates = [i for i in range(1, count) if given[i] < largest] or [i for i in range(1, count) if given[i] < most]
        mass, left = sum([loads[i] for i in candidates]), surplus
        for i in candidates:
            addition = min(most - given[i], max(1, left * loads[i] // mass), surplus)
            given[i] = given[i] + addition
            surplus = surplus - addition
    return np.array(given)


def centred(stream_key, shape, spread, most, pieces=(), kind=jnp.bfloat16):
    gain = block_levels(stream_key, shape, pieces, -0.22, 0.18) if pieces else 1.0
    values = jax.random.normal(stream_key, shape, jnp.float32) * spread * gain
    return jnp.minimum(jnp.maximum(values, -most), most).astype(kind)


def setup_inputs(seed: int = 0) -> dict:
    arg_keys = jax.random.split(jax.random.key(seed), 11)
    source = centred(arg_keys[0], (2, NZ, NY, NX), 1.0, 6.0, ((1, 8), (2, 8), (3, 8)), jnp.float32)
    adjoint_start = centred(arg_keys[1], (2, NZ, NY, NX), 0.5, 4.0, ((1, 8), (2, 8), (3, 8)), jnp.float32)
    couple = jnp.clip(jnp.exp(math.log(2.4) - 2.7725887 * jax.random.uniform(arg_keys[2], (6, NZ, NY, NX), jnp.float32) ** block_levels(arg_keys[2], (6, NZ, NY, NX), ((1, 8), (2, 8), (3, 8)), -0.2, 0.2)), 0.15, 2.4)
    diag_inverse = jnp.clip(jnp.exp(math.log(0.16) - 0.4700036 * jax.random.uniform(arg_keys[3], (2, NZ, NY, NX), jnp.float32) ** block_levels(arg_keys[3], (2, NZ, NY, NX), ((1, 8), (2, 8), (3, 8)), -0.2, 0.2)), 0.1, 0.16)
    cross_inverse = jnp.clip(jax.random.uniform(arg_keys[4], (2, NZ, NY, NX), jnp.float32, -0.04, 0.04) * block_levels(arg_keys[4], (2, NZ, NY, NX), ((1, 8), (2, 8), (3, 8)), -0.4, 0.0), -0.04, 0.04)
    perf_row = draw_perf_row(jax.random.fold_in(arg_keys[10], 71), 0)
    well_owner_keys = jax.random.split(jax.random.fold_in(arg_keys[6], 1), ZDEVS * YDEVS * XDEVS * PANELS // PANELS)
    well_owner_turns = jax.random.permutation(jax.random.fold_in(arg_keys[6], 3), ZDEVS * YDEVS * XDEVS * PANELS // PANELS)
    well_owner = jax.vmap(lambda own, number: assign_block(jax.random.fold_in(arg_keys[6], 2), own, number, PANELS, YDEVS * XDEVS, 1, CAP, 2))(well_owner_keys, well_owner_turns).reshape((ZDEVS, YDEVS, XDEVS, PANELS, 1))
    well_slot = set_ends(jax.random.randint(arg_keys[7], (ZDEVS, YDEVS, XDEVS, PANELS), 0, WELL_DEV), jax.random.fold_in(arg_keys[7], 1), 0, WELL_DEV - 1).astype(jnp.int32)
    well_block = centred(arg_keys[8], (ZDEVS, YDEVS, XDEVS, WELL_DEV, 2 * CX, 2 * CX), (2 * CX) ** -0.5, 0.375, ((0, 8), (1, 8), (2, 8)))
    cross_block = centred(arg_keys[9], (ZDEVS, YDEVS, XDEVS, WELL_DEV, 2 * CX, 2 * CX), (2 * CX * PANELS // WELL_DEV) ** -0.5, 0.09375, ((0, 8), (1, 8), (2, 8)))
    return {"source": source, "adjoint_start": adjoint_start, "couple": couple, "diag_inverse": diag_inverse, "cross_inverse": cross_inverse, "perf_row": perf_row, "well_owner": well_owner, "well_slot": well_slot, "well_block": well_block, "cross_block": cross_block}


def neighbours(padded, couple):
    summed = couple[0] * padded[:, 2:, 1:-1, 1:-1]
    summed = summed + couple[1] * padded[:, :-2, 1:-1, 1:-1]
    summed = summed + couple[2] * padded[:, 1:-1, 2:, 1:-1]
    summed = summed + couple[3] * padded[:, 1:-1, :-2, 1:-1]
    summed = summed + couple[4] * padded[:, 1:-1, 1:-1, 2:]
    summed = summed + couple[5] * padded[:, 1:-1, 1:-1, :-2]
    return summed


def jacobi_sweep(padded, right_side, couple, diag_inverse, cross_inverse):
    inflow = right_side + neighbours(padded, couple)
    first_comp = diag_inverse[0] * inflow[0] + cross_inverse[0] * inflow[1]
    second_comp = cross_inverse[1] * inflow[0] + diag_inverse[1] * inflow[1]
    return jnp.stack([first_comp, second_comp])


def to_blocks(field_all):
    shaped = field_all.reshape(2, ZDEVS, CZ, YDEVS, CY, XDEVS, CX)
    return shaped.transpose(1, 3, 5, 0, 2, 4, 6).reshape(ZDEVS, YDEVS, XDEVS, 2, CZ * CY, CX)


def from_blocks(blocks):
    shaped = blocks.reshape(ZDEVS, YDEVS, XDEVS, 2, CZ, CY, CX)
    return shaped.transpose(3, 0, 4, 1, 5, 2, 6).reshape(2, NZ, NY, NX)


def well_source(adjoint, perf_row, well_owner, well_slot, well_block, cross_block):
    blocks = to_blocks(adjoint)
    row_index = jnp.broadcast_to(perf_row[:, :, :, None, :, None], (ZDEVS, YDEVS, XDEVS, 2, PANELS, CX)).astype(jnp.int32)
    picked = jnp.take_along_axis(blocks, row_index, axis=4)
    owners = YDEVS * XDEVS
    well_count = owners * WELL_DEV
    panels = picked.transpose(0, 1, 2, 4, 3, 5).reshape(ZDEVS, owners * PANELS, 2 * CX).astype(jnp.bfloat16)
    well_ids = (well_owner[..., 0] * WELL_DEV + well_slot).reshape(ZDEVS, owners * PANELS).astype(jnp.int32)
    well_mats = well_block.reshape(ZDEVS, well_count, 2 * CX, 2 * CX)
    cross_mats = cross_block.reshape(ZDEVS, well_count, 2 * CX, 2 * CX)

    def per_slab(slab_args):
        slab_panels, slab_ids, slab_mats, slab_cross = slab_args
        totals = jax.ops.segment_sum(slab_panels.astype(jnp.float32), slab_ids, num_segments=well_count).astype(jnp.bfloat16)
        crossed = jnp.einsum('wd,wde->we', totals.astype(jnp.float32), slab_cross.astype(jnp.float32), precision=lax.Precision.HIGHEST)

        def per_owner(group_args):
            group_panels, group_ids = group_args
            chosen = slab_mats[group_ids].astype(jnp.float32)
            return jnp.einsum('pd,pde->pe', group_panels.astype(jnp.float32), chosen, precision=lax.Precision.HIGHEST)

        own_term = lax.map(per_owner, (slab_panels.reshape(owners, PANELS, 2 * CX), slab_ids.reshape(owners, PANELS)))
        own_term = own_term.reshape(owners * PANELS, 2 * CX)
        return (own_term + crossed[slab_ids]).astype(jnp.bfloat16)

    responses = lax.map(per_slab, (panels, well_ids, well_mats, cross_mats))
    values = responses.astype(jnp.float32).reshape(ZDEVS, YDEVS, XDEVS, PANELS, 2, CX).transpose(0, 1, 2, 4, 3, 5)
    selector = (perf_row[..., None, :] == jnp.arange(CZ * CY, dtype=jnp.int32)[:, None]).astype(jnp.float32)
    placed = jnp.einsum('zyxrp,zyxcpw->zyxcrw', selector, values, precision=lax.Precision.HIGHEST)
    return from_blocks(placed)


def reference(source, adjoint_start, couple, diag_inverse, cross_inverse, perf_row, well_owner, well_slot, well_block, cross_block):
    adjoint = adjoint_start
    for outer_step in range(OUTER):
        right_side = source + well_source(adjoint, perf_row, well_owner, well_slot, well_block, cross_block)
        for sweep_step in range(SWEEPS):
            padded = jnp.pad(adjoint, ((0, 0), (1, 1), (1, 1), (1, 1)))
            adjoint = jacobi_sweep(padded, right_side, couple, diag_inverse, cross_inverse)
    return adjoint
```

```python
import jax
import jax.numpy as jnp
from jax import lax
from jax.experimental import pallas as pl
from jax.experimental.pallas import tpu as pltpu
from jax.sharding import PartitionSpec as P

SWEEPS = 4
OUTER = 2
F32 = jnp.float32
BF16 = jnp.bfloat16
NZ, NY, NX = 8, 32, 128
EZ, EY, EX = 16, 40, 256
OWNERS = 64
SLOTS = 128
COEFS = 12
CZ = 14


def iota(shape, dim):
    return lax.broadcasted_iota(jnp.int32, shape, dim)


def call(body, out_shape, scratch=(), limit=32):
    return pl.pallas_call(
        body,
        out_shape=out_shape,
        scratch_shapes=list(scratch),
        compiler_params=pltpu.CompilerParams(vmem_limit_bytes=limit * 1024 * 1024),
    )


def dot(a, b):
    return jnp.dot(a.astype(BF16), b.astype(BF16), preferred_element_type=F32)


def panels_body(adj, perf, owner, slot, out, sc):
    own = owner[...].astype(F32)
    i0, i1 = iota((64, 64), 0), iota((64, 64), 1)
    wide = jnp.broadcast_to(own, (64, 64))
    tall = jnp.sum(jnp.where(i0 == i1, wide, 0.0), axis=1, keepdims=True)
    rank = jnp.sum(jnp.where((tall == wide) & (i0 < i1), 1.0, 0.0), axis=0, keepdims=True)
    dest = rank * float(OWNERS) + own
    hit = iota((SLOTS, 64), 0).astype(F32) == dest
    row_code = jnp.sum(jnp.where(hit, perf[...].astype(F32) + 1.0, 0.0), axis=1, keepdims=True)
    slot_code = jnp.sum(jnp.where(hit, slot[...].astype(F32) + 1.0, 0.0), axis=1, keepdims=True)
    pick = jnp.where(row_code == (iota((SLOTS, 256), 1) + 1).astype(F32), 1.0, 0.0)
    lane = iota((SLOTS, 128), 1)
    meta = jnp.where(lane == 0, slot_code, jnp.where(lane == 1, row_code, 0.0))
    for c in range(2):
        picked = dot(pick, adj[c].reshape(NZ * NY, NX))
        for k in range(2):
            sc[pl.ds(2 * c + k, 64, stride=8), :] = picked[k * 64 : (k + 1) * 64]
    zero = jnp.zeros((64, 128), F32)
    for k in range(2):
        sc[pl.ds(4 + k, 64, stride=8), :] = meta[k * 64 : (k + 1) * 64]
        sc[pl.ds(6 + k, 64, stride=8), :] = zero
    out[...] = sc[...].astype(BF16)


def panels(adj, perf, owner, slot):
    return call(
        panels_body,
        jax.ShapeDtypeStruct((512, 128), BF16),
        [pltpu.VMEM((512, 128), F32)],
    )(adj, perf, owner, slot)


def owner_body(arrived, well, cross, out, sx, rq):
    sx[...] = arrived[...].astype(F32)

    def rows(i):
        return jnp.concatenate(
            [sx[pl.ds(i, 64, stride=8), :], sx[pl.ds(i + 1, 64, stride=8), :]], axis=0
        )

    meta = rows(4)
    ident, row_code = meta[:, 0:1], meta[:, 1:2]
    panel = jnp.concatenate([rows(0), rows(2)], axis=1)
    i0, i1 = iota((SLOTS, SLOTS), 0), iota((SLOTS, SLOTS), 1)
    across = jnp.sum(jnp.where(i0 == i1, ident, 0.0), axis=0, keepdims=True)
    same = jnp.where(ident == across, 1.0, 0.0)
    totals = dot(same, panel).astype(BF16).astype(F32)
    mixed = jnp.zeros((SLOTS, 256), F32)
    for w in range(4):
        mine = ident == float(w + 1)
        mixed = mixed + dot(jnp.where(mine, panel, 0.0), well[w])
        mixed = mixed + dot(jnp.where(mine, totals, 0.0), cross[w])
    mixed = mixed.astype(BF16).astype(F32)
    tag = jnp.where(iota((SLOTS, 128), 1) == 96, row_code, 0.0)
    for k in range(2):
        part = slice(k * 64, (k + 1) * 64)
        for c in range(2):
            rq[pl.ds(2 * c + k, 64, stride=8), :] = mixed[part, c * 128 : (c + 1) * 128]
        rq[pl.ds(4 + k, 64, stride=8), :] = tag[part]
        rq[pl.ds(6 + k, 64, stride=8), :] = jnp.zeros((64, 128), F32)
    full = rq[...].reshape(64, 8, 128)
    sub, lane = iota((64, 8, 128), 1), iota((64, 8, 128), 2)

    def from_y(v, step):
        gap = jnp.zeros((8, 8, 128), F32)
        return jnp.concatenate([gap, v[:-8]] if step < 0 else [v[8:], gap], axis=0)

    def from_x(v, step):
        v = v.reshape(8, 8, 8, 128)
        gap = jnp.zeros((8, 1, 8, 128), F32)
        v = jnp.concatenate([gap, v[:, :-1]] if step < 0 else [v[:, 1:], gap], axis=1)
        return v.reshape(64, 8, 128)

    def turn(v, by):
        return pltpu.roll(v, by, 2)

    def half(v):
        return pltpu.roll(v, 4, 1)

    below, above = from_y(full, -1), from_y(full, 1)
    edge = jnp.where(lane >= 125, from_x(full, -1), jnp.where(lane < 3, from_x(full, 1), 0.0))
    edges = edge + turn(from_y(edge, -1), 32) + turn(from_y(edge, 1), 64)
    tags = jnp.where((sub >= 4) & (lane == 96), full, 0.0)
    tags = tags + turn(from_y(tags, -1), 1) + turn(from_y(tags, 1), 2)
    tags = tags + turn(from_x(tags, -1), 3) + turn(from_x(tags, 1), 6)
    first = jnp.where(sub < 4, full, half(below))
    second = jnp.where(sub < 4, above, half(jnp.where(sub < 4, edges, 0.0)) + tags)
    out[...] = jnp.concatenate([first, second], axis=1).astype(BF16)


def owner_work(arrived, well, cross):
    return call(
        owner_body,
        jax.ShapeDtypeStruct((64, 16, 128), BF16),
        [pltpu.VMEM((512, 128), F32), pltpu.VMEM((512, 128), F32)],
    )(arrived, well, cross)


def place_body(arrived, ws, up, down, sx):
    sx[...] = arrived[...].reshape(1024, 128).astype(F32)

    def rows(i):
        return jnp.concatenate(
            [sx[pl.ds(i, 64, stride=16), :], sx[pl.ds(i + 1, 64, stride=16), :]], axis=0
        )

    def both(i):
        return jnp.concatenate([rows(i), rows(i + 2)], axis=1)

    codes = rows(12).T

    def code(n):
        return codes[96 + n : 97 + n, :]

    def place(want, n, values):
        return dot(jnp.where(want == code(n), 1.0, 0.0), values)

    lane = jnp.bitwise_and(iota((SLOTS, 256), 1), 127)

    def sides(by):
        v = jnp.concatenate(
            [pltpu.roll(rows(12), by, 1) if by else rows(12), pltpu.roll(rows(14), by, 1) if by else rows(14)],
            axis=1,
        )
        return jnp.where(lane >= 125, v, 0.0), jnp.where(lane < 3, v, 0.0)

    own = (iota((256, SLOTS), 0) + 1).astype(F32)
    g = iota((64, SLOTS), 0)
    j = jnp.bitwise_and(g, 7)
    base = (g - j) * 4 + j + 1
    high = jnp.where(j < 3, base, -1).astype(F32)
    low = jnp.where(j >= 5, base + 24, -1).astype(F32)
    main = place(own, 0, both(0))
    halo = place(low, 1, both(4)) + place(high, 2, both(8))
    minus, plus = sides(0)
    side = place(own, 3, minus) + place(own, 6, plus)
    minus, plus = sides(96)
    corner = place(low, 4, minus) + place(low, 7, plus)
    minus, plus = sides(64)
    corner = corner + place(high, 5, minus) + place(high, 8, plus)
    for c in range(2):
        part = slice(c * 128, (c + 1) * 128)
        ws[c, :, 0:32, 0:128] = main[:, part].reshape(8, 32, 128)
        ws[c, :, 32:40, 0:128] = halo[:, part].reshape(8, 8, 128)
        ws[c, :, 0:32, 128:256] = side[:, part].reshape(8, 32, 128)
        ws[c, :, 32:40, 128:256] = corner[:, part].reshape(8, 8, 128)
        up[c] = ws[c, 5:8].astype(BF16)
        down[c] = ws[c, 0:3].astype(BF16)


def place(arrived):
    return call(
        place_body,
        (
            jax.ShapeDtypeStruct((2, NZ, EY, EX), F32),
            jax.ShapeDtypeStruct((2, 3, EY, EX), BF16),
            jax.ShapeDtypeStruct((2, 3, EY, EX), BF16),
        ),
        [pltpu.VMEM((1024, 128), F32)],
    )(arrived)


def fields_of(refs):
    couple, diag, cross, source = refs
    return [(couple, i) for i in range(6)] + [(r, i) for r in (diag, cross, source) for i in range(2)]


def zsend_body(*refs):
    ins, (up, down) = refs[:-2], refs[-2:]
    adj = ins[0]
    for c in range(2):
        up[4 * c : 4 * c + 4] = adj[c, 4:8].astype(BF16)
        down[4 * c : 4 * c + 4] = adj[c, 0:4].astype(BF16)
    if len(ins) > 1:
        for n, (ref, i) in enumerate(fields_of(ins[1:])):
            up[8 + 3 * n : 11 + 3 * n] = ref[i, 5:8].astype(BF16)
            down[8 + 3 * n : 11 + 3 * n] = ref[i, 0:3].astype(BF16)


def zsend(*ins):
    planes = 44 if len(ins) > 1 else 8
    shape = jax.ShapeDtypeStruct((planes, NY, NX), BF16)
    return call(zsend_body, (shape, shape))(*ins)


def adj_plane(adj, zlo, zhi, c, z):
    if z < 4:
        return zlo[4 * c + z].astype(F32)
    if z >= 12:
        return zhi[4 * c + z - 12].astype(F32)
    return adj[c, z - 4]


def coef_plane(ref, i, n, zlo, zhi, e):
    if e < 3:
        return zlo[8 + 3 * n + e].astype(F32)
    if e >= 11:
        return zhi[8 + 3 * n + e - 11].astype(F32)
    return ref[i, e - 3]


def ysend_body(*refs):
    ins, (zlo, zhi, up, down) = refs[:-4], refs[-4:]
    low = iota((8, 128), 0) < 4

    def pack(index, even, odd):
        up[index] = jnp.where(low, pltpu.roll(even[24:32], 4, 0), odd[24:32]).astype(BF16)
        down[index] = jnp.where(low, even[0:8], pltpu.roll(odd[0:8], 4, 0)).astype(BF16)

    for c in range(2):
        for h in range(8):
            pack(8 * c + h, *[adj_plane(ins[0], zlo, zhi, c, 2 * h + o) for o in range(2)])
    if len(ins) > 1:
        for n, (ref, i) in enumerate(fields_of(ins[1:])):
            for h in range(7):
                pack(16 + 7 * n + h, *[coef_plane(ref, i, n, zlo, zhi, 2 * h + o) for o in range(2)])


def ysend(*ins):
    tiles = 100 if len(ins) > 3 else 16
    shape = jax.ShapeDtypeStruct((tiles, 8, 128), BF16)
    return call(ysend_body, (shape, shape))(*ins)


def y_tiles(ylo, yhi, index):
    low = iota((8, 128), 0) < 4
    a, b = ylo[index].astype(F32), yhi[index].astype(F32)
    even = jnp.where(low, b, pltpu.roll(a, 4, 0))
    odd = jnp.where(low, pltpu.roll(b, 4, 0), a)
    return even, odd


def xsend_body(*refs):
    ins, (zlo, zhi, ylo, yhi, out) = refs[:-5], refs[-5:]
    group = lax.shift_right_logical(iota((8, 128), 1), 3)
    group4 = lax.shift_right_logical(iota((32, 128), 1), 3)

    def pack(index, count, plane, tile_at):
        acc = jnp.zeros((32, 128), F32)
        edge = jnp.zeros((8, 128), F32)
        for h in range(count // 2):
            tiles = y_tiles(ylo, yhi, tile_at + h)
            for o in range(2):
                z = 2 * h + o
                acc = jnp.where(group4 == z, pltpu.roll(plane(z), 8 * z + 4 if z < 15 else 124, 1), acc)
                edge = jnp.where(group == z, pltpu.roll(tiles[o], 8 * z + 4, 1), edge)
        out[index, 0:32] = acc.astype(BF16)
        out[index, 32:40] = edge.astype(BF16)

    for c in range(2):
        pack(c, EZ, lambda z, c=c: adj_plane(ins[0], zlo, zhi, c, z), 8 * c)
    if len(ins) > 1:
        for n, (ref, i) in enumerate(fields_of(ins[1:])):
            pack(
                2 + n,
                CZ,
                lambda e, n=n, ref=ref, i=i: coef_plane(ref, i, n, zlo, zhi, e),
                16 + 7 * n,
            )


def xsend(*ins):
    fields = 14 if len(ins) > 5 else 2
    return call(xsend_body, jax.ShapeDtypeStruct((fields, EY, 128), BF16))(*ins)


def sweeps_body(
    adj, couple, diag, cross, source,
    azlo, azhi, aylo, ayhi, axlo, axhi,
    czlo, czhi, cylo, cyhi, cxlo, cxhi,
    ws, wlo, whi,
    out, field, bufs, rhs,
):
    lane = iota((EY, 128), 1)
    from_low = jnp.bitwise_and(lane, 7) < 4
    keep = (lane < 4) | (lane >= 124)

    def columns(xlo, xhi, index):
        return jnp.where(from_low, xlo[index].astype(F32), xhi[index].astype(F32))

    def spread(packed, z):
        return jnp.where(keep, pltpu.roll(packed, (124 - 8 * z) % 128, 1), 0.0)

    for c in range(2):
        packed = columns(axlo, axhi, c)
        for h in range(8):
            tiles = y_tiles(aylo, ayhi, 8 * c + h)
            for o in range(2):
                z = 2 * h + o
                bufs[0, c, z, 0:32, 0:128] = adj_plane(adj, azlo, azhi, c, z)
                bufs[0, c, z, 32:40, 0:128] = tiles[o]
                bufs[0, c, z, :, 128:256] = spread(packed, z)
    for n, (ref, i) in enumerate(fields_of((couple, diag, cross, source))):
        packed = columns(cxlo, cxhi, 2 + n)
        for h in range(7):
            tiles = y_tiles(cylo, cyhi, 16 + 7 * n + h)
            for o in range(2):
                e = 2 * h + o
                field[n, e, 0:32, 0:128] = coef_plane(ref, i, n, czlo, czhi, e)
                field[n, e, 32:40, 0:128] = tiles[o]
                field[n, e, :, 128:256] = spread(packed, e)
    for c in range(2):
        for e in range(CZ):
            if e < 3:
                extra = wlo[c, e].astype(F32)
            elif e >= 11:
                extra = whi[c, e - 11].astype(F32)
            else:
                extra = ws[c, e - 3]
            rhs[c, e] = field[10 + c, e] + extra

    for s in range(SWEEPS):
        last = s == SWEEPS - 1
        rows, lanes = (NY, NX) if last else (EY, EX)

        def layer(z, carry, s=s, last=last, rows=rows, lanes=lanes):
            e = z - 1
            src = s % 2

            def co(n):
                return field[n, e, 0:rows, 0:lanes]

            inflow = []
            for c in range(2):
                here = bufs[src, c, z]
                total = rhs[c, e, 0:rows, 0:lanes]
                total = total + co(0) * bufs[src, c, z + 1, 0:rows, 0:lanes]
                total = total + co(1) * bufs[src, c, z - 1, 0:rows, 0:lanes]
                total = total + co(2) * pltpu.roll(here, EY - 1, 0)[0:rows, 0:lanes]
                total = total + co(3) * pltpu.roll(here, 1, 0)[0:rows, 0:lanes]
                total = total + co(4) * pltpu.roll(here, EX - 1, 1)[0:rows, 0:lanes]
                total = total + co(5) * pltpu.roll(here, 1, 1)[0:rows, 0:lanes]
                inflow.append(total)
            new0 = co(6) * inflow[0] + co(8) * inflow[1]
            new1 = co(9) * inflow[0] + co(7) * inflow[1]
            if last:
                out[0, z - 4] = new0
                out[1, z - 4] = new1
            else:
                bufs[1 - src, 0, z] = new0
                bufs[1 - src, 1, z] = new1
            return carry

        lax.fori_loop(1 + s, EZ - 1 - s, layer, 0)


def sweeps(*ins):
    return call(
        sweeps_body,
        jax.ShapeDtypeStruct((2, NZ, NY, NX), F32),
        [
            pltpu.VMEM((COEFS, CZ, EY, EX), F32),
            pltpu.VMEM((2, 2, EZ, EY, EX), F32),
            pltpu.VMEM((2, CZ, EY, EX), F32),
        ],
    )(*ins)


def exchange(up, down, axis):
    count = lax.axis_size(axis)
    forward = [(i, i + 1) for i in range(count - 1)]
    backward = [(i + 1, i) for i in range(count - 1)]
    return lax.ppermute(up, axis, forward), lax.ppermute(down, axis, backward)


def per_device(
    source,
    adjoint_start,
    couple,
    diag_inverse,
    cross_inverse,
    perf_row,
    well_owner,
    well_slot,
    well_block,
    cross_block,
):
    perf = perf_row.reshape(1, -1)
    owner = well_owner.reshape(1, -1)
    slot = well_slot.reshape(1, -1)
    well = well_block.reshape(well_block.shape[3:])
    cross_mats = cross_block.reshape(cross_block.shape[3:])
    fields = (couple, diag_inverse, cross_inverse, source)
    adjoint = adjoint_start
    kept = None
    for outer_step in range(OUTER):
        more = fields if outer_step == 0 else ()
        sent = panels(adjoint, perf, owner, slot)
        arrived = lax.all_to_all(sent, ("gy", "gx"), split_axis=0, concat_axis=0, tiled=True)
        zlo, zhi = exchange(*zsend(adjoint, *more), "gz")
        ylo, yhi = exchange(*ysend(adjoint, *more, zlo, zhi), "gy")
        packed = xsend(adjoint, *more, zlo, zhi, ylo, yhi)
        xlo, xhi = exchange(packed, packed, "gx")
        halo = (zlo, zhi, ylo, yhi, xlo, xhi)
        kept = halo if kept is None else kept
        answers = owner_work(arrived, well, cross_mats)
        returned = lax.all_to_all(answers, ("gy", "gx"), split_axis=0, concat_axis=0, tiled=True)
        ws, up, down = place(returned)
        wlo, whi = exchange(up, down, "gz")
        adjoint = sweeps(adjoint, *fields, *halo, *kept, ws, wlo, whi)
    return adjoint


def solution(mesh):
    placed = (
        P(None, "gz", "gy", "gx"),
        P(None, "gz", "gy", "gx"),
        P(None, "gz", "gy", "gx"),
        P(None, "gz", "gy", "gx"),
        P(None, "gz", "gy", "gx"),
        P("gz", "gy", "gx", None),
        P("gz", "gy", "gx", None, None),
        P("gz", "gy", "gx", None),
        P("gz", "gy", "gx", None, None, None),
        P("gz", "gy", "gx", None, None, None),
    )
    return jax.shard_map(
        per_device, mesh=mesh, in_specs=placed, out_specs=P(None, "gz", "gy", "gx"), check_vma=False
    )
```

```python
import jax
import jax.numpy as jnp
from jax import lax
from jax.experimental import pallas as pl
from jax.experimental.pallas import tpu as pltpu
from jax.sharding import PartitionSpec as P

SWEEPS = 4
OUTER = 2
F32 = jnp.float32
BF16 = jnp.bfloat16
NZ, NY, NX = 8, 32, 128
EZ, EY = 16, 40
OWNERS = 64
SLOTS = 128
CZ = 14


def iota(shape, dim):
    return lax.broadcasted_iota(jnp.int32, shape, dim)


def call(body, out_shape, scratch=(), limit=32):
    return pl.pallas_call(
        body,
        out_shape=out_shape,
        scratch_shapes=list(scratch),
        compiler_params=pltpu.CompilerParams(vmem_limit_bytes=limit * 1024 * 1024),
    )


def dot(a, b):
    return jnp.dot(a.astype(BF16), b.astype(BF16), preferred_element_type=F32)


def y_tiles(ylo, yhi, index):
    low = iota((8, 128), 0) < 4
    a, b = ylo[index].astype(F32), yhi[index].astype(F32)
    even = jnp.where(low, b, pltpu.roll(a, 4, 0))
    odd = jnp.where(low, pltpu.roll(b, 4, 0), a)
    return even, odd


def columns(xlo, xhi, index):
    low = jnp.bitwise_and(iota((EY, 128), 1), 7) < 4
    return jnp.where(low, xlo[index].astype(F32), xhi[index].astype(F32))


def lane_group():
    return lax.shift_right_logical(iota((EY, 128), 1), 3)


def to_strip(plane, z, strip):
    return jnp.where(lane_group() == z, pltpu.roll(plane, 8 * z + 4, 1), strip)


def tall(main, tile):
    return jnp.concatenate([main, tile], axis=0)


def panels_body(adj, perf, owner, slot, out, sc):
    own = owner[...].astype(F32)
    i0, i1 = iota((64, 64), 0), iota((64, 64), 1)
    wide = jnp.broadcast_to(own, (64, 64))
    down = jnp.sum(jnp.where(i0 == i1, wide, 0.0), axis=1, keepdims=True)
    rank = jnp.sum(jnp.where((down == wide) & (i0 < i1), 1.0, 0.0), axis=0, keepdims=True)
    dest = rank * float(OWNERS) + own
    hit = iota((SLOTS, 64), 0).astype(F32) == dest
    row_code = jnp.sum(jnp.where(hit, perf[...].astype(F32) + 1.0, 0.0), axis=1, keepdims=True)
    slot_code = jnp.sum(jnp.where(hit, slot[...].astype(F32) + 1.0, 0.0), axis=1, keepdims=True)
    pick = jnp.where(row_code == (iota((SLOTS, 256), 1) + 1).astype(F32), 1.0, 0.0)
    lane = iota((SLOTS, 128), 1)
    meta = jnp.where(lane == 0, slot_code, jnp.where(lane == 1, row_code, 0.0))
    for c in range(2):
        picked = dot(pick, adj[c].reshape(NZ * NY, NX))
        for k in range(2):
            sc[pl.ds(2 * c + k, 64, stride=8), :] = picked[k * 64 : (k + 1) * 64]
    zero = jnp.zeros((64, 128), F32)
    for k in range(2):
        sc[pl.ds(4 + k, 64, stride=8), :] = meta[k * 64 : (k + 1) * 64]
        sc[pl.ds(6 + k, 64, stride=8), :] = zero
    out[...] = sc[...].astype(BF16)


def panels(adj, perf, owner, slot):
    return call(
        panels_body,
        jax.ShapeDtypeStruct((512, 128), BF16),
        [pltpu.VMEM((512, 128), F32)],
    )(adj, perf, owner, slot)


def owner_body(arrived, well, cross, out, sx, rq):
    sx[...] = arrived[...].astype(F32)

    def rows(i):
        return jnp.concatenate(
            [sx[pl.ds(i, 64, stride=8), :], sx[pl.ds(i + 1, 64, stride=8), :]], axis=0
        )

    meta = rows(4)
    ident, row_code = meta[:, 0:1], meta[:, 1:2]
    panel = jnp.concatenate([rows(0), rows(2)], axis=1)
    i0, i1 = iota((SLOTS, SLOTS), 0), iota((SLOTS, SLOTS), 1)
    across = jnp.sum(jnp.where(i0 == i1, ident, 0.0), axis=0, keepdims=True)
    same = jnp.where(ident == across, 1.0, 0.0)
    totals = dot(same, panel).astype(BF16).astype(F32)
    mixed = jnp.zeros((SLOTS, 256), F32)
    for w in range(4):
        mine = ident == float(w + 1)
        mixed = mixed + dot(jnp.where(mine, panel, 0.0), well[w])
        mixed = mixed + dot(jnp.where(mine, totals, 0.0), cross[w])
    mixed = mixed.astype(BF16).astype(F32)
    tag = jnp.where(iota((SLOTS, 128), 1) == 96, row_code, 0.0)
    for k in range(2):
        part = slice(k * 64, (k + 1) * 64)
        for c in range(2):
            rq[pl.ds(2 * c + k, 64, stride=8), :] = mixed[part, c * 128 : (c + 1) * 128]
        rq[pl.ds(4 + k, 64, stride=8), :] = tag[part]
        rq[pl.ds(6 + k, 64, stride=8), :] = jnp.zeros((64, 128), F32)
    full = rq[...].reshape(64, 8, 128)
    sub, lane = iota((64, 8, 128), 1), iota((64, 8, 128), 2)

    def from_y(v, step):
        gap = jnp.zeros((8, 8, 128), F32)
        return jnp.concatenate([gap, v[:-8]] if step < 0 else [v[8:], gap], axis=0)

    def from_x(v, step):
        v = v.reshape(8, 8, 8, 128)
        gap = jnp.zeros((8, 1, 8, 128), F32)
        v = jnp.concatenate([gap, v[:, :-1]] if step < 0 else [v[:, 1:], gap], axis=1)
        return v.reshape(64, 8, 128)

    def turn(v, by):
        return pltpu.roll(v, by, 2)

    def half(v):
        return pltpu.roll(v, 4, 1)

    below, above = from_y(full, -1), from_y(full, 1)
    edge = jnp.where(lane >= 125, from_x(full, -1), jnp.where(lane < 3, from_x(full, 1), 0.0))
    edges = edge + turn(from_y(edge, -1), 32) + turn(from_y(edge, 1), 64)
    tags = jnp.where((sub >= 4) & (lane == 96), full, 0.0)
    tags = tags + turn(from_y(tags, -1), 1) + turn(from_y(tags, 1), 2)
    tags = tags + turn(from_x(tags, -1), 3) + turn(from_x(tags, 1), 6)
    first = jnp.where(sub < 4, full, half(below))
    second = jnp.where(sub < 4, above, half(jnp.where(sub < 4, edges, 0.0)) + tags)
    out[...] = jnp.concatenate([first, second], axis=1).astype(BF16)


def owner_work(arrived, well, cross):
    return call(
        owner_body,
        jax.ShapeDtypeStruct((64, 16, 128), BF16),
        [pltpu.VMEM((512, 128), F32), pltpu.VMEM((512, 128), F32)],
    )(arrived, well, cross)


def place_body(arrived, *refs):
    ins, (ws, wx, up, down, sx) = refs[:-5], refs[-5:]
    sx[...] = arrived[...].reshape(1024, 128).astype(F32)

    def rows(i):
        return jnp.concatenate(
            [sx[pl.ds(i, 64, stride=16), :], sx[pl.ds(i + 1, 64, stride=16), :]], axis=0
        )

    def both(i):
        return jnp.concatenate([rows(i), rows(i + 2)], axis=1)

    codes = rows(12).T

    def code(n):
        return codes[96 + n : 97 + n, :]

    def place(want, n, values):
        return dot(jnp.where(want == code(n), 1.0, 0.0), values)

    lane = jnp.bitwise_and(iota((SLOTS, 256), 1), 127)

    def sides(by):
        v = jnp.concatenate(
            [pltpu.roll(rows(12), by, 1) if by else rows(12), pltpu.roll(rows(14), by, 1) if by else rows(14)],
            axis=1,
        )
        return jnp.where(lane >= 125, v, 0.0), jnp.where(lane < 3, v, 0.0)

    own = (iota((256, SLOTS), 0) + 1).astype(F32)
    g = iota((64, SLOTS), 0)
    j = jnp.bitwise_and(g, 7)
    base = (g - j) * 4 + j + 1
    high = jnp.where(j < 3, base, -1).astype(F32)
    low = jnp.where(j >= 5, base + 24, -1).astype(F32)
    main = place(own, 0, both(0))
    halo = place(low, 1, both(4)) + place(high, 2, both(8))
    minus, plus = sides(0)
    side = place(own, 3, minus) + place(own, 6, plus)
    minus, plus = sides(96)
    corner = place(low, 4, minus) + place(low, 7, plus)
    minus, plus = sides(64)
    corner = corner + place(high, 5, minus) + place(high, 8, plus)
    for c in range(2):
        part = slice(c * 128, (c + 1) * 128)
        main_c = main[:, part].reshape(8, 32, 128)
        halo_c = halo[:, part].reshape(8, 8, 128)
        side_c = side[:, part].reshape(8, 32, 128)
        corner_c = corner[:, part].reshape(8, 8, 128)
        strip = jnp.zeros((EY, 128), F32)
        for z in range(NZ):
            ws[c, z] = tall(main_c[z], halo_c[z])
            strip = to_strip(tall(side_c[z], corner_c[z]), z + 4, strip)
        wx[c] = strip
        first = 4 if ins else 0
        for ref, z0, w0 in ((up, 4, 5), (down, 0, 0)):
            packed = jnp.where(
                (lane_group() >= first) & (lane_group() < first + 3),
                pltpu.roll(strip, (8 * (first - w0 - 4)) % 128, 1),
                0.0,
            )
            if ins:
                adj, ylo, yhi, xlo, xhi = ins
                cols = columns(xlo, xhi, c)
                cols = pltpu.roll(cols, 128 - 8 * z0, 1) if z0 else cols
                packed = jnp.where(lane_group() < 4, cols, packed)
                for h in range(2):
                    tiles = y_tiles(ylo, yhi, 4 * c + z0 // 2 + h)
                    for o in range(2):
                        ref[c, 2 * h + o] = tall(adj[c, z0 + 2 * h + o], tiles[o]).astype(BF16)
            for j in range(3):
                ref[c, first + j] = tall(main_c[w0 + j], halo_c[w0 + j]).astype(BF16)
            ref[c, first + 3] = packed.astype(BF16)


def place(arrived, *ins):
    sent = jax.ShapeDtypeStruct((2, 8 if ins else 4, EY, 128), BF16)
    return call(
        place_body,
        (
            jax.ShapeDtypeStruct((2, NZ, EY, 128), F32),
            jax.ShapeDtypeStruct((2, EY, 128), F32),
            sent,
            sent,
        ),
        [pltpu.VMEM((1024, 128), F32)],
    )(arrived, *ins)


def fields_of(refs):
    out = [(refs[0], 0), (refs[0], 1)]
    if len(refs) > 1:
        out += [(refs[1], i) for i in range(6)]
        out += [(r, i) for r in refs[2:5] for i in range(2)]
    return out


def ysend_body(*refs):
    ins, (up, down) = refs[:-2], refs[-2:]
    low = iota((8, 128), 0) < 4
    for f, (ref, i) in enumerate(fields_of(ins)):
        for h in range(4):
            z = 2 * h
            up[4 * f + h] = jnp.where(
                low, pltpu.roll(ref[i, z, 24:32], 4, 0), ref[i, z + 1, 24:32]
            ).astype(BF16)
            down[4 * f + h] = jnp.where(
                low, ref[i, z, 0:8], pltpu.roll(ref[i, z + 1, 0:8], 4, 0)
            ).astype(BF16)


def ysend(*ins):
    shape = jax.ShapeDtypeStruct((56 if len(ins) > 1 else 8, 8, 128), BF16)
    return call(ysend_body, (shape, shape))(*ins)


def block_planes(ref, i, f, ylo, yhi):
    planes = []
    for h in range(4):
        tiles = y_tiles(ylo, yhi, 4 * f + h)
        planes += [tall(ref[i, 2 * h + o], tiles[o]) for o in range(2)]
    return planes


def z_slot(f):
    return (4 * f, 4) if f < 2 else (3 * f + 2, 3)


def zsend_body(*refs):
    ins, (ylo, yhi, up, down) = refs[:-4], refs[-4:]
    for f, (ref, i) in enumerate(fields_of(ins)):
        planes = block_planes(ref, i, f, ylo, yhi)
        at, deep = z_slot(f)
        for j in range(deep):
            up[at + j] = planes[NZ - deep + j].astype(BF16)
            down[at + j] = planes[j].astype(BF16)


def zsend(*ins):
    shape = jax.ShapeDtypeStruct((44, EY, NX), BF16)
    return call(zsend_body, (shape, shape))(*ins)


def field_planes(ref, i, f, ylo, yhi, zlo, zhi):
    at, deep = z_slot(f)
    low = [zlo[at + j].astype(F32) for j in range(deep)]
    high = [zhi[at + j].astype(F32) for j in range(deep)]
    return low + block_planes(ref, i, f, ylo, yhi) + high


def xsend_body(*refs):
    if len(refs) == 4:
        adj, ylo, yhi, out = refs
        for c in range(2):
            strip = jnp.zeros((EY, 128), F32)
            for z, plane in enumerate(block_planes(adj, c, c, ylo, yhi)):
                strip = to_strip(plane, z, strip)
            out[c] = strip.astype(BF16)
        return
    ins, (ylo, yhi, zlo, zhi, out) = refs[:-5], refs[-5:]
    for f, (ref, i) in enumerate(fields_of(ins)):
        strip = jnp.zeros((EY, 128), F32)
        for z, plane in enumerate(field_planes(ref, i, f, ylo, yhi, zlo, zhi)):
            strip = to_strip(plane, z + (f >= 2), strip)
        out[f] = strip.astype(BF16)


def xsend(*ins):
    fields = 14 if len(ins) > 3 else 2
    return call(xsend_body, jax.ShapeDtypeStruct((fields, EY, 128), BF16))(*ins)


def sweeps_body(*refs):
    ins, ylo, yhi, zlo, zhi, xlo, xhi = refs[:5], *refs[5:11]
    out, field, fstrip, buf0, buf1, overs, rhs, rstrip = refs[-8:]
    ws, wx, wlo, whi = refs[-12:-8]
    later = refs[11:-12]
    bufs = (buf0, buf1)
    strips = []
    skip = 4 if later else 0
    group = lane_group()
    lane = iota((EY, 128), 1)
    column = jnp.bitwise_and(lane, 7)

    for c in range(2):
        ends = [r[c, skip + 3].astype(F32) for r in (wlo, whi)]
        if later:
            yl, yh, xl, xh = later
            planes = [wlo[c, j].astype(F32) for j in range(4)]
            planes += block_planes(ins[0], c, c, yl, yh)
            planes += [whi[c, j].astype(F32) for j in range(4)]
            strip = pltpu.roll(columns(xl, xh, c), 32, 1)
            strip = jnp.where(group < 4, ends[0], strip)
            strip = jnp.where(group >= 12, pltpu.roll(ends[1], 96, 1), strip)
        else:
            planes = field_planes(ins[0], c, c, ylo, yhi, zlo, zhi)
            strip = columns(xlo, xhi, c)
        for z, plane in enumerate(planes):
            buf0[c, z] = plane
        strips.append(strip)
        side = wx[c]
        side = jnp.where(group < 4, pltpu.roll(ends[0], (8 - 8 * skip) % 128, 1), side)
        side = jnp.where(group >= 12, pltpu.roll(ends[1], 96 - 8 * skip, 1), side)
        rstrip[c] = side + columns(xlo, xhi, 12 + c)
        for e, plane in enumerate(field_planes(ins[4], c, 12 + c, ylo, yhi, zlo, zhi)):
            if e < 3:
                extra = wlo[c, skip + e].astype(F32)
            elif e >= 11:
                extra = whi[c, skip + e - 11].astype(F32)
            else:
                extra = ws[c, e - 3]
            rhs[c, e] = plane + extra
    for n, (ref, i) in enumerate(fields_of(ins)[2:12]):
        for e, plane in enumerate(field_planes(ref, i, n + 2, ylo, yhi, zlo, zhi)):
            field[n, e] = plane
        fstrip[n] = columns(xlo, xhi, n + 2)

    def mix(co, inflow):
        return co(6) * inflow[0] + co(8) * inflow[1], co(9) * inflow[0] + co(7) * inflow[1]

    for s in range(SWEEPS):
        last = s == SWEEPS - 1
        src, dst = bufs[s % 2], bufs[1 - s % 2]
        rows = NY if last else EY
        layers = range(1 + s, EZ - 1 - s)
        edges = []
        for c in range(2):
            edge = jnp.zeros((EY, 128), F32)
            for z in layers:
                overs[c, z] = pltpu.roll(strips[c], 124 - 8 * z, 1)
                if not last:
                    edge = to_strip(src[c, z], z, edge)
            edges.append(edge)

        for z in layers:

            def co(n):
                return field[n, z - 1, 0:rows]

            inflow = []
            for c in range(2):
                here, over = src[c, z], overs[c, z]
                right = pltpu.roll(jnp.where(lane == 0, over, here), 127, 1)
                left = pltpu.roll(jnp.where(lane == 127, over, here), 1, 1)
                total = rhs[c, z - 1, 0:rows]
                total = total + co(0) * src[c, z + 1, 0:rows]
                total = total + co(1) * src[c, z - 1, 0:rows]
                total = total + co(2) * pltpu.roll(here, EY - 1, 0)[0:rows]
                total = total + co(3) * pltpu.roll(here, 1, 0)[0:rows]
                total = total + co(4) * right[0:rows]
                total = total + co(5) * left[0:rows]
                inflow.append(total)
            for c, new in enumerate(mix(co, inflow)):
                if last:
                    out[c, z - 4] = new
                else:
                    dst[c, z] = new
        if last:
            continue

        def co(n):
            return fstrip[n]

        inflow = []
        for c in range(2):
            here, edge = strips[c], edges[c]
            right = pltpu.roll(jnp.where(column == 4, edge, here), 127, 1)
            left = pltpu.roll(jnp.where(column == 3, edge, here), 1, 1)
            total = rstrip[c]
            total = total + co(0) * pltpu.roll(here, 120, 1) + co(1) * pltpu.roll(here, 8, 1)
            total = total + co(2) * pltpu.roll(here, EY - 1, 0) + co(3) * pltpu.roll(here, 1, 0)
            total = total + co(4) * right + co(5) * left
            inflow.append(total)
        strips = list(mix(co, inflow))


def sweeps(*ins):
    return call(
        sweeps_body,
        jax.ShapeDtypeStruct((2, NZ, NY, NX), F32),
        [
            pltpu.VMEM((10, CZ, EY, 128), F32),
            pltpu.VMEM((10, EY, 128), F32),
            pltpu.VMEM((2, EZ, EY, 128), F32),
            pltpu.VMEM((2, EZ, EY, 128), F32),
            pltpu.VMEM((2, EZ, EY, 128), F32),
            pltpu.VMEM((2, CZ, EY, 128), F32),
            pltpu.VMEM((2, EY, 128), F32),
        ],
    )(*ins)


def exchange(up, down, axis):
    count = lax.axis_size(axis)
    forward = [(i, i + 1) for i in range(count - 1)]
    backward = [(i + 1, i) for i in range(count - 1)]
    return lax.ppermute(up, axis, forward), lax.ppermute(down, axis, backward)


def per_device(
    source,
    adjoint_start,
    couple,
    diag_inverse,
    cross_inverse,
    perf_row,
    well_owner,
    well_slot,
    well_block,
    cross_block,
):
    perf = perf_row.reshape(1, -1)
    owner = well_owner.reshape(1, -1)
    slot = well_slot.reshape(1, -1)
    well = well_block.reshape(well_block.shape[3:])
    cross_mats = cross_block.reshape(cross_block.shape[3:])
    fields = (couple, diag_inverse, cross_inverse, source)
    start = (adjoint_start, *fields)
    sent = panels(adjoint_start, perf, owner, slot)
    arrived = lax.all_to_all(sent, ("gy", "gx"), split_axis=0, concat_axis=0, tiled=True)
    ylo, yhi = exchange(*ysend(*start), "gy")
    zlo, zhi = exchange(*zsend(*start, ylo, yhi), "gz")
    packed = xsend(*start, ylo, yhi, zlo, zhi)
    kept = (*fields, ylo, yhi, zlo, zhi, *exchange(packed, packed, "gx"))
    answers = owner_work(arrived, well, cross_mats)
    returned = lax.all_to_all(answers, ("gy", "gx"), split_axis=0, concat_axis=0, tiled=True)
    ws, wx, up, down = place(returned)
    adjoint = sweeps(adjoint_start, *kept, ws, wx, *exchange(up, down, "gz"))

    for _ in range(OUTER - 1):
        sent = panels(adjoint, perf, owner, slot)
        arrived = lax.all_to_all(sent, ("gy", "gx"), split_axis=0, concat_axis=0, tiled=True)
        ylo, yhi = exchange(*ysend(adjoint), "gy")
        arrived, ylo, yhi = lax.optimization_barrier((arrived, ylo, yhi))
        packed = xsend(adjoint, ylo, yhi)
        answers = owner_work(arrived, well, cross_mats)
        returned = lax.all_to_all(answers, ("gy", "gx"), split_axis=0, concat_axis=0, tiled=True)
        halo = (ylo, yhi, *exchange(packed, packed, "gx"))
        ws, wx, up, down = place(returned, adjoint, *halo)
        adjoint = sweeps(adjoint, *kept, *halo, ws, wx, *exchange(up, down, "gz"))
    return adjoint


def solution(mesh):
    placed = (
        P(None, "gz", "gy", "gx"),
        P(None, "gz", "gy", "gx"),
        P(None, "gz", "gy", "gx"),
        P(None, "gz", "gy", "gx"),
        P(None, "gz", "gy", "gx"),
        P("gz", "gy", "gx", None),
        P("gz", "gy", "gx", None, None),
        P("gz", "gy", "gx", None),
        P("gz", "gy", "gx", None, None, None),
        P("gz", "gy", "gx", None, None, None),
    )
    return jax.shard_map(
        per_device, mesh=mesh, in_specs=placed, out_specs=P(None, "gz", "gy", "gx"), check_vma=False
    )
```

```python
import jax
import jax.numpy as jnp
from jax import lax
from jax.experimental import pallas as pl
from jax.experimental.pallas import tpu as pltpu
from jax.sharding import PartitionSpec as P

SWEEPS = 4
OUTER = 2
F32 = jnp.float32
BF16 = jnp.bfloat16
NZ, NY, NX = 8, 32, 128
EZ, EY = 16, 40
OWNERS = 64
SLOTS = 128
CZ = 14


def iota(shape, dim):
    return lax.broadcasted_iota(jnp.int32, shape, dim)


def call(body, out_shape, scratch=(), far=None):
    specs, limit = {}, 32
    if far is not None:
        limit = 58 if far[-1] else 32
        specs["in_specs"] = [pl.BlockSpec(memory_space=pl.ANY if f else pltpu.VMEM) for f in far]
    return pl.pallas_call(
        body,
        out_shape=out_shape,
        scratch_shapes=list(scratch),
        compiler_params=pltpu.CompilerParams(vmem_limit_bytes=limit * 1024 * 1024),
        **specs,
    )


def start_copies(pairs, sems):
    copies = [pltpu.make_async_copy(a, b, sems.at[i]) for i, (a, b) in enumerate(pairs)]
    for copy in copies:
        copy.start()
    return copies


def dot(a, b):
    return jnp.dot(a.astype(BF16), b.astype(BF16), preferred_element_type=F32)


def y_tiles(ylo, yhi, index):
    low = iota((8, 128), 0) < 4
    a, b = ylo[index].astype(F32), yhi[index].astype(F32)
    even = jnp.where(low, b, pltpu.roll(a, 4, 0))
    odd = jnp.where(low, pltpu.roll(b, 4, 0), a)
    return even, odd


def columns(xlo, xhi, index):
    low = jnp.bitwise_and(iota((EY, 128), 1), 7) < 4
    return jnp.where(low, xlo[index].astype(F32), xhi[index].astype(F32))


def lane_group():
    return lax.shift_right_logical(iota((EY, 128), 1), 3)


def to_strip(plane, z, strip):
    return jnp.where(lane_group() == z, pltpu.roll(plane, 8 * z + 4, 1), strip)


def tall(main, tile):
    return jnp.concatenate([main, tile], axis=0)


def panels_body(perf, owner, slot, adj, out, sc, *near):
    far = len(near) > 0
    if far:
        near, sems = near
        (copy,) = start_copies([(adj, near)], sems)
    own = owner[...].astype(F32)
    i0, i1 = iota((64, 64), 0), iota((64, 64), 1)
    wide = jnp.broadcast_to(own, (64, 64))
    down = jnp.sum(jnp.where(i0 == i1, wide, 0.0), axis=1, keepdims=True)
    rank = jnp.sum(jnp.where((down == wide) & (i0 < i1), 1.0, 0.0), axis=0, keepdims=True)
    dest = rank * float(OWNERS) + own
    hit = iota((SLOTS, 64), 0).astype(F32) == dest
    row_code = jnp.sum(jnp.where(hit, perf[...].astype(F32) + 1.0, 0.0), axis=1, keepdims=True)
    slot_code = jnp.sum(jnp.where(hit, slot[...].astype(F32) + 1.0, 0.0), axis=1, keepdims=True)
    pick = jnp.where(row_code == (iota((SLOTS, 256), 1) + 1).astype(F32), 1.0, 0.0)
    lane = iota((SLOTS, 128), 1)
    meta = jnp.where(lane == 0, slot_code, jnp.where(lane == 1, row_code, 0.0))
    if far:
        copy.wait()
        adj = near
    for c in range(2):
        picked = dot(pick, adj[c].reshape(NZ * NY, NX))
        for k in range(2):
            sc[pl.ds(2 * c + k, 64, stride=8), :] = picked[k * 64 : (k + 1) * 64]
    zero = jnp.zeros((64, 128), F32)
    for k in range(2):
        sc[pl.ds(4 + k, 64, stride=8), :] = meta[k * 64 : (k + 1) * 64]
        sc[pl.ds(6 + k, 64, stride=8), :] = zero
    out[...] = sc[...].astype(BF16)


def panels(adj, perf, owner, slot, far=False):
    near = [pltpu.VMEM(adj.shape, F32), pltpu.SemaphoreType.DMA((1,))] if far else []
    return call(
        panels_body,
        jax.ShapeDtypeStruct((512, 128), BF16),
        [pltpu.VMEM((512, 128), F32), *near],
        (False, False, False, far),
    )(perf, owner, slot, adj)


def owner_body(arrived, well, cross, out, sx, rq):
    sx[...] = arrived[...].astype(F32)

    def rows(i):
        return jnp.concatenate(
            [sx[pl.ds(i, 64, stride=8), :], sx[pl.ds(i + 1, 64, stride=8), :]], axis=0
        )

    meta = rows(4)
    ident, row_code = meta[:, 0:1], meta[:, 1:2]
    panel = jnp.concatenate([rows(0), rows(2)], axis=1)
    i0, i1 = iota((SLOTS, SLOTS), 0), iota((SLOTS, SLOTS), 1)
    across = jnp.sum(jnp.where(i0 == i1, ident, 0.0), axis=0, keepdims=True)
    same = jnp.where(ident == across, 1.0, 0.0)
    totals = dot(same, panel).astype(BF16).astype(F32)
    mixed = jnp.zeros((SLOTS, 256), F32)
    for w in range(4):
        mine = ident == float(w + 1)
        mixed = mixed + dot(jnp.where(mine, panel, 0.0), well[w])
        mixed = mixed + dot(jnp.where(mine, totals, 0.0), cross[w])
    mixed = mixed.astype(BF16).astype(F32)
    tag = jnp.where(iota((SLOTS, 128), 1) == 96, row_code, 0.0)
    for k in range(2):
        part = slice(k * 64, (k + 1) * 64)
        for c in range(2):
            rq[pl.ds(2 * c + k, 64, stride=8), :] = mixed[part, c * 128 : (c + 1) * 128]
        rq[pl.ds(4 + k, 64, stride=8), :] = tag[part]
        rq[pl.ds(6 + k, 64, stride=8), :] = jnp.zeros((64, 128), F32)
    full = rq[...].reshape(64, 8, 128)
    sub, lane = iota((64, 8, 128), 1), iota((64, 8, 128), 2)

    def from_y(v, step):
        gap = jnp.zeros((8, 8, 128), F32)
        return jnp.concatenate([gap, v[:-8]] if step < 0 else [v[8:], gap], axis=0)

    def from_x(v, step):
        v = v.reshape(8, 8, 8, 128)
        gap = jnp.zeros((8, 1, 8, 128), F32)
        v = jnp.concatenate([gap, v[:, :-1]] if step < 0 else [v[:, 1:], gap], axis=1)
        return v.reshape(64, 8, 128)

    def turn(v, by):
        return pltpu.roll(v, by, 2)

    def half(v):
        return pltpu.roll(v, 4, 1)

    below, above = from_y(full, -1), from_y(full, 1)
    edge = jnp.where(lane >= 125, from_x(full, -1), jnp.where(lane < 3, from_x(full, 1), 0.0))
    edges = edge + turn(from_y(edge, -1), 32) + turn(from_y(edge, 1), 64)
    tags = jnp.where((sub >= 4) & (lane == 96), full, 0.0)
    tags = tags + turn(from_y(tags, -1), 1) + turn(from_y(tags, 1), 2)
    tags = tags + turn(from_x(tags, -1), 3) + turn(from_x(tags, 1), 6)
    first = jnp.where(sub < 4, full, half(below))
    second = jnp.where(sub < 4, above, half(jnp.where(sub < 4, edges, 0.0)) + tags)
    out[...] = jnp.concatenate([first, second], axis=1).astype(BF16)


def owner_work(arrived, well, cross):
    return call(
        owner_body,
        jax.ShapeDtypeStruct((64, 16, 128), BF16),
        [pltpu.VMEM((512, 128), F32), pltpu.VMEM((512, 128), F32)],
    )(arrived, well, cross)


def place_body(arrived, *refs):
    ins, (ws, wx, up, down, sx) = refs[:-5], refs[-5:]
    sx[...] = arrived[...].reshape(1024, 128).astype(F32)

    def rows(i):
        return jnp.concatenate(
            [sx[pl.ds(i, 64, stride=16), :], sx[pl.ds(i + 1, 64, stride=16), :]], axis=0
        )

    def both(i):
        return jnp.concatenate([rows(i), rows(i + 2)], axis=1)

    codes = rows(12).T

    def code(n):
        return codes[96 + n : 97 + n, :]

    def place(want, n, values):
        return dot(jnp.where(want == code(n), 1.0, 0.0), values)

    lane = jnp.bitwise_and(iota((SLOTS, 256), 1), 127)

    def sides(by):
        v = jnp.concatenate(
            [pltpu.roll(rows(12), by, 1) if by else rows(12), pltpu.roll(rows(14), by, 1) if by else rows(14)],
            axis=1,
        )
        return jnp.where(lane >= 125, v, 0.0), jnp.where(lane < 3, v, 0.0)

    own = (iota((256, SLOTS), 0) + 1).astype(F32)
    g = iota((64, SLOTS), 0)
    j = jnp.bitwise_and(g, 7)
    base = (g - j) * 4 + j + 1
    high = jnp.where(j < 3, base, -1).astype(F32)
    low = jnp.where(j >= 5, base + 24, -1).astype(F32)
    main = place(own, 0, both(0))
    halo = place(low, 1, both(4)) + place(high, 2, both(8))
    minus, plus = sides(0)
    side = place(own, 3, minus) + place(own, 6, plus)
    minus, plus = sides(96)
    corner = place(low, 4, minus) + place(low, 7, plus)
    minus, plus = sides(64)
    corner = corner + place(high, 5, minus) + place(high, 8, plus)
    for c in range(2):
        part = slice(c * 128, (c + 1) * 128)
        main_c = main[:, part].reshape(8, 32, 128)
        halo_c = halo[:, part].reshape(8, 8, 128)
        side_c = side[:, part].reshape(8, 32, 128)
        corner_c = corner[:, part].reshape(8, 8, 128)
        strip = jnp.zeros((EY, 128), F32)
        for z in range(NZ):
            ws[c, z] = tall(main_c[z], halo_c[z])
            strip = to_strip(tall(side_c[z], corner_c[z]), z + 4, strip)
        wx[c] = strip
        first = 4 if ins else 0
        for ref, z0, w0 in ((up, 4, 5), (down, 0, 0)):
            packed = jnp.where(
                (lane_group() >= first) & (lane_group() < first + 3),
                pltpu.roll(strip, (8 * (first - w0 - 4)) % 128, 1),
                0.0,
            )
            if ins:
                adj, ylo, yhi, xlo, xhi = ins
                cols = pltpu.roll(columns(xlo, xhi, 0), -8 * (8 * c + z0) % 128, 1)
                packed = jnp.where(lane_group() < 4, cols, packed)
                for h in range(2):
                    tiles = y_tiles(ylo, yhi, 4 * c + z0 // 2 + h)
                    for o in range(2):
                        ref[c, 2 * h + o] = tall(adj[c, z0 + 2 * h + o], tiles[o]).astype(BF16)
            for j in range(3):
                ref[c, first + j] = tall(main_c[w0 + j], halo_c[w0 + j]).astype(BF16)
            ref[c, first + 3] = packed.astype(BF16)


def place(arrived, *ins):
    sent = jax.ShapeDtypeStruct((2, 8 if ins else 4, EY, 128), BF16)
    return call(
        place_body,
        (
            jax.ShapeDtypeStruct((2, NZ, EY, 128), F32),
            jax.ShapeDtypeStruct((2, EY, 128), F32),
            sent,
            sent,
        ),
        [pltpu.VMEM((1024, 128), F32)],
    )(arrived, *ins)


def fields_of(refs):
    out = [(refs[0], 0), (refs[0], 1)]
    if len(refs) > 1:
        out += [(refs[1], i) for i in range(6)]
        out += [(r, i) for r in refs[2:5] for i in range(2)]
    return out


def ysend_body(*refs):
    high = 24
    if len(refs) == 3:
        ins, (up, down) = refs[:1], refs[1:]
    else:
        far, (up, down), ins, sems = refs[:5], refs[5:7], refs[7:12], refs[12]
        high = 8
        pairs = [(a.at[:, :, 0:8], b.at[:, :, 0:8]) for a, b in zip(far, ins)]
        pairs += [(a.at[:, :, 24:32], b.at[:, :, 8:16]) for a, b in zip(far, ins)]
        for copy in start_copies(pairs, sems):
            copy.wait()
    low = iota((8, 128), 0) < 4
    for f, (ref, i) in enumerate(fields_of(ins)):
        for h in range(4):
            z = 2 * h
            up[4 * f + h] = jnp.where(
                low, pltpu.roll(ref[i, z, high : high + 8], 4, 0), ref[i, z + 1, high : high + 8]
            ).astype(BF16)
            down[4 * f + h] = jnp.where(
                low, ref[i, z, 0:8], pltpu.roll(ref[i, z + 1, 0:8], 4, 0)
            ).astype(BF16)


def ysend(*ins):
    shape = jax.ShapeDtypeStruct((56 if len(ins) > 1 else 8, 8, 128), BF16)
    near = []
    if len(ins) > 1:
        near = [pltpu.VMEM((a.shape[0], NZ, 16, NX), F32) for a in ins]
        near += [pltpu.SemaphoreType.DMA((2 * len(ins),))]
    return call(ysend_body, (shape, shape), near, [len(ins) > 1] * len(ins))(*ins)


def block_planes(ref, i, f, ylo, yhi):
    planes = []
    for h in range(4):
        tiles = y_tiles(ylo, yhi, 4 * f + h)
        planes += [tall(ref[i, 2 * h + o], tiles[o]) for o in range(2)]
    return planes


def z_slot(f):
    return (4 * f, 4) if f < 2 else (3 * f + 2, 3)


def zsend_body(*refs):
    ins, (ylo, yhi, xlo, xhi, up, down) = refs[:-6], refs[-6:]
    group = lane_group()
    for f, (ref, i) in enumerate(fields_of(ins)):
        planes = block_planes(ref, i, f, ylo, yhi)
        at, deep = z_slot(f)
        for j in range(deep):
            up[at + j] = planes[NZ - deep + j].astype(BF16)
            down[at + j] = planes[j].astype(BF16)
    for q in range(4):
        for out, top in ((up, True), (down, False)):
            strip = jnp.zeros((EY, 128), F32)
            for f in range(4 * q, min(4 * q + 4, 14)):
                to = 4 * (f % 4)
                came = 8 * (f % 2) + (NZ - z_slot(f)[1] if top else 0)
                moved = pltpu.roll(columns(xlo, xhi, f // 2), 8 * (to - came) % 128, 1)
                strip = jnp.where((group >= to) & (group < to + 4), moved, strip)
            out[44 + q] = strip.astype(BF16)


def zsend(*ins):
    shape = jax.ShapeDtypeStruct((48, EY, NX), BF16)
    return call(zsend_body, (shape, shape))(*ins)


def field_planes(ref, i, f, ylo, yhi, zlo, zhi):
    at, deep = z_slot(f)
    low = [zlo[at + j].astype(F32) for j in range(deep)]
    high = [zhi[at + j].astype(F32) for j in range(deep)]
    return low + block_planes(ref, i, f, ylo, yhi) + high


def join_strips(low, mid, high):
    group = lane_group()
    return jnp.where(group < 4, low, jnp.where(group < 12, mid, high))


def block_strip(xlo, xhi, f):
    return pltpu.roll(columns(xlo, xhi, f // 2), 8 * (4 - 8 * (f % 2)) % 128, 1)


def field_strip(f, xlo, xhi, zlo, zhi):
    deep, at = z_slot(f)[1], 4 * (f % 4)
    low = pltpu.roll(zlo[44 + f // 4].astype(F32), 8 * (4 - deep - at) % 128, 1)
    high = pltpu.roll(zhi[44 + f // 4].astype(F32), 8 * (12 - at) % 128, 1)
    return join_strips(low, block_strip(xlo, xhi, f), high)


def xsend_body(*refs):
    ins, (ylo, yhi, out) = refs[:-3], refs[-3:]
    strip = None
    for f, (ref, i) in enumerate(fields_of(ins)):
        strip = strip if f % 2 else jnp.zeros((EY, 128), F32)
        for z, plane in enumerate(block_planes(ref, i, f, ylo, yhi)):
            strip = to_strip(plane, z + 8 * (f % 2), strip)
        if f % 2:
            out[f // 2] = strip.astype(BF16)


def xsend(*ins):
    return call(xsend_body, jax.ShapeDtypeStruct((7 if len(ins) > 3 else 1, EY, 128), BF16))(*ins)


def sweeps_body(*refs):
    ins, ylo, yhi, xlo, xhi, zlo, zhi = refs[:5], *refs[5:11]
    out, field, fstrip, buf0, buf1, overs, rhs, rstrip = refs[-8:]
    ws, wx, wlo, whi = refs[-12:-8]
    later = refs[11:-12]
    bufs = (buf0, buf1)
    strips = []
    skip = 4 if later else 0
    lane = iota((EY, 128), 1)
    column = jnp.bitwise_and(lane, 7)

    for c in range(2):
        if later:
            planes = [wlo[c, j].astype(F32) for j in range(4)]
            planes += block_planes(ins[0], c, c, *later[:2])
            planes += [whi[c, j].astype(F32) for j in range(4)]
        else:
            planes = field_planes(ins[0], c, c, ylo, yhi, zlo, zhi)
        for z, plane in enumerate(planes):
            buf0[c, z] = plane
        for e, plane in enumerate(field_planes(ins[4], c, 12 + c, ylo, yhi, zlo, zhi)):
            if e < 3:
                extra = wlo[c, skip + e].astype(F32)
            elif e >= 11:
                extra = whi[c, skip + e - 11].astype(F32)
            else:
                extra = ws[c, e - 3]
            rhs[c, e] = plane + extra
    for n, (ref, i) in enumerate(fields_of(ins)[2:12]):
        for e, plane in enumerate(field_planes(ref, i, n + 2, ylo, yhi, zlo, zhi)):
            field[n, e] = plane
    for n in range(10):
        fstrip[n] = field_strip(n + 2, xlo, xhi, zlo, zhi)
    for c in range(2):
        ends = [r[c, skip + 3].astype(F32) for r in (wlo, whi)]
        if later:
            strip = join_strips(ends[0], block_strip(*later[2:], c), pltpu.roll(ends[1], 96, 1))
        else:
            strip = field_strip(c, xlo, xhi, zlo, zhi)
        strips.append(strip)
        side = join_strips(
            pltpu.roll(ends[0], (8 - 8 * skip) % 128, 1), wx[c], pltpu.roll(ends[1], 96 - 8 * skip, 1)
        )
        rstrip[c] = side + field_strip(12 + c, xlo, xhi, zlo, zhi)

    def mix(co, inflow):
        return co(6) * inflow[0] + co(8) * inflow[1], co(9) * inflow[0] + co(7) * inflow[1]

    for s in range(SWEEPS):
        last = s == SWEEPS - 1
        src, dst = bufs[s % 2], bufs[1 - s % 2]
        rows = NY if last else EY
        layers = range(1 + s, EZ - 1 - s)
        edges = []
        for c in range(2):
            edge = jnp.zeros((EY, 128), F32)
            for z in layers:
                overs[c, z] = pltpu.roll(strips[c], 124 - 8 * z, 1)
                if not last:
                    edge = to_strip(src[c, z], z, edge)
            edges.append(edge)

        for z in layers:

            def co(n):
                return field[n, z - 1, 0:rows]

            inflow = []
            for c in range(2):
                here, over = src[c, z], overs[c, z]
                right = pltpu.roll(jnp.where(lane == 0, over, here), 127, 1)
                left = pltpu.roll(jnp.where(lane == 127, over, here), 1, 1)
                total = rhs[c, z - 1, 0:rows]
                total = total + co(0) * src[c, z + 1, 0:rows]
                total = total + co(1) * src[c, z - 1, 0:rows]
                total = total + co(2) * pltpu.roll(here, EY - 1, 0)[0:rows]
                total = total + co(3) * pltpu.roll(here, 1, 0)[0:rows]
                total = total + co(4) * right[0:rows]
                total = total + co(5) * left[0:rows]
                inflow.append(total)
            for c, new in enumerate(mix(co, inflow)):
                if last:
                    out[c, z - 4] = new
                else:
                    dst[c, z] = new
        if last:
            continue

        def co(n):
            return fstrip[n]

        inflow = []
        for c in range(2):
            here, edge = strips[c], edges[c]
            right = pltpu.roll(jnp.where(column == 4, edge, here), 127, 1)
            left = pltpu.roll(jnp.where(column == 3, edge, here), 1, 1)
            total = rstrip[c]
            total = total + co(0) * pltpu.roll(here, 120, 1) + co(1) * pltpu.roll(here, 8, 1)
            total = total + co(2) * pltpu.roll(here, EY - 1, 0) + co(3) * pltpu.roll(here, 1, 0)
            total = total + co(4) * right + co(5) * left
            inflow.append(total)
        strips = list(mix(co, inflow))


def sweeps(*ins):
    return call(
        sweeps_body,
        jax.ShapeDtypeStruct((2, NZ, NY, NX), F32),
        [
            pltpu.VMEM((10, CZ, EY, 128), F32),
            pltpu.VMEM((10, EY, 128), F32),
            pltpu.VMEM((2, EZ, EY, 128), F32),
            pltpu.VMEM((2, EZ, EY, 128), F32),
            pltpu.VMEM((2, EZ, EY, 128), F32),
            pltpu.VMEM((2, CZ, EY, 128), F32),
            pltpu.VMEM((2, EY, 128), F32),
        ],
    )(*ins)


def exchange(up, down, axis):
    count = lax.axis_size(axis)
    forward = [(i, i + 1) for i in range(count - 1)]
    backward = [(i + 1, i) for i in range(count - 1)]
    return lax.ppermute(up, axis, forward), lax.ppermute(down, axis, backward)


def per_device(
    source,
    adjoint_start,
    couple,
    diag_inverse,
    cross_inverse,
    perf_row,
    well_owner,
    well_slot,
    well_block,
    cross_block,
):
    perf = perf_row.reshape(1, -1)
    owner = well_owner.reshape(1, -1)
    slot = well_slot.reshape(1, -1)
    well = well_block.reshape(well_block.shape[3:])
    cross_mats = cross_block.reshape(cross_block.shape[3:])
    fields = (couple, diag_inverse, cross_inverse, source)
    start = (adjoint_start, *fields)
    sent = panels(adjoint_start, perf, owner, slot, far=True)
    arrived = lax.all_to_all(sent, ("gy", "gx"), split_axis=0, concat_axis=0, tiled=True)
    ylo, yhi = exchange(*ysend(*start), "gy")
    packed = xsend(*start, ylo, yhi)
    halo = (ylo, yhi, *exchange(packed, packed, "gx"))
    kept = (*fields, *halo, *exchange(*zsend(*start, *halo), "gz"))
    answers = owner_work(arrived, well, cross_mats)
    returned = lax.all_to_all(answers, ("gy", "gx"), split_axis=0, concat_axis=0, tiled=True)
    ws, wx, up, down = place(returned)
    adjoint = sweeps(adjoint_start, *kept, ws, wx, *exchange(up, down, "gz"))

    for _ in range(OUTER - 1):
        sent = panels(adjoint, perf, owner, slot)
        arrived = lax.all_to_all(sent, ("gy", "gx"), split_axis=0, concat_axis=0, tiled=True)
        ylo, yhi = exchange(*ysend(adjoint), "gy")
        arrived, ylo, yhi = lax.optimization_barrier((arrived, ylo, yhi))
        packed = xsend(adjoint, ylo, yhi)
        answers = owner_work(arrived, well, cross_mats)
        returned = lax.all_to_all(answers, ("gy", "gx"), split_axis=0, concat_axis=0, tiled=True)
        halo = (ylo, yhi, *exchange(packed, packed, "gx"))
        ws, wx, up, down = place(returned, adjoint, *halo)
        adjoint = sweeps(adjoint, *kept, *halo, ws, wx, *exchange(up, down, "gz"))
    return adjoint


def solution(mesh):
    placed = (
        P(None, "gz", "gy", "gx"),
        P(None, "gz", "gy", "gx"),
        P(None, "gz", "gy", "gx"),
        P(None, "gz", "gy", "gx"),
        P(None, "gz", "gy", "gx"),
        P("gz", "gy", "gx", None),
        P("gz", "gy", "gx", None, None),
        P("gz", "gy", "gx", None),
        P("gz", "gy", "gx", None, None, None),
        P("gz", "gy", "gx", None, None, None),
    )
    return jax.shard_map(
        per_device, mesh=mesh, in_specs=placed, out_specs=P(None, "gz", "gy", "gx"), check_vma=False
    )
```

```python
import functools

import jax
import jax.numpy as jnp
from jax import lax
from jax.experimental import pallas as pl
from jax.experimental.pallas import tpu as pltpu
from jax.sharding import PartitionSpec as P

SWEEPS = 4
F32 = jnp.float32
BF16 = jnp.bfloat16
NZ, NY, NX = 8, 32, 128
EZ, EY = 16, 48
OWNERS = 64
SLOTS = 128
CZ = 14


def iota(shape, dim):
    return lax.broadcasted_iota(jnp.int32, shape, dim)


def call(body, out_shape, scratch=(), far=None):
    specs, limit = {}, 32
    if far is not None:
        limit = 58 if all(far) else 32
        specs["in_specs"] = [pl.BlockSpec(memory_space=pl.ANY if f else pltpu.VMEM) for f in far]
    return pl.pallas_call(
        body,
        out_shape=out_shape,
        scratch_shapes=list(scratch),
        compiler_params=pltpu.CompilerParams(vmem_limit_bytes=limit * 1024 * 1024),
        **specs,
    )


def start_copies(pairs, sems):
    copies = [pltpu.make_async_copy(a, b, sems.at[i]) for i, (a, b) in enumerate(pairs)]
    for copy in copies:
        copy.start()
    return copies


def dot(a, b):
    return jnp.dot(a.astype(BF16), b.astype(BF16), preferred_element_type=F32)


def lane_group():
    return lax.shift_right_logical(iota((EY, 128), 1), 4)


def columns(xlo, xhi, index):
    low = jnp.bitwise_and(iota((EY, 128), 1), 15) < 8
    return jnp.where(low, xlo[index].astype(F32), xhi[index].astype(F32))


def to_strip(plane, g, strip):
    return jnp.where(lane_group() == g, pltpu.roll(plane, 16 * g + 8, 1), strip)


def swap(strip):
    return pltpu.roll(strip, 64, 1)


def by_half(low, high):
    return jnp.where(lane_group() < 4, low, high)


def tall(main, above, below):
    return jnp.concatenate([main, above, below], axis=0)


def panels_body(perf, owner, slot, adj, out, sc, *near):
    far = len(near) > 0
    if far:
        near, sems = near
        (copy,) = start_copies([(adj, near)], sems)
    own = owner[...].astype(F32)
    i0, i1 = iota((64, 64), 0), iota((64, 64), 1)
    wide = jnp.broadcast_to(own, (64, 64))
    down = jnp.sum(jnp.where(i0 == i1, wide, 0.0), axis=1, keepdims=True)
    rank = jnp.sum(jnp.where((down == wide) & (i0 < i1), 1.0, 0.0), axis=0, keepdims=True)
    dest = rank * float(OWNERS) + own
    hit = iota((SLOTS, 64), 0).astype(F32) == dest
    row_code = jnp.sum(jnp.where(hit, perf[...].astype(F32) + 1.0, 0.0), axis=1, keepdims=True)
    slot_code = jnp.sum(jnp.where(hit, slot[...].astype(F32) + 1.0, 0.0), axis=1, keepdims=True)
    pick = jnp.where(row_code == (iota((SLOTS, 256), 1) + 1).astype(F32), 1.0, 0.0)
    lane = iota((SLOTS, 128), 1)
    meta = jnp.where(lane == 0, slot_code, jnp.where(lane == 1, row_code, 0.0))
    if far:
        copy.wait()
        adj = near
    for c in range(2):
        picked = dot(pick, adj[c, :, 0:NY].reshape(NZ * NY, NX))
        for k in range(2):
            sc[pl.ds(2 * c + k, 64, stride=8), :] = picked[k * 64 : (k + 1) * 64]
    zero = jnp.zeros((64, 128), F32)
    for k in range(2):
        sc[pl.ds(4 + k, 64, stride=8), :] = meta[k * 64 : (k + 1) * 64]
        sc[pl.ds(6 + k, 64, stride=8), :] = zero
    out[...] = sc[...].astype(BF16)


def panels(adj, perf, owner, slot, far=False):
    near = [pltpu.VMEM(adj.shape, F32), pltpu.SemaphoreType.DMA((1,))] if far else []
    return call(
        panels_body,
        jax.ShapeDtypeStruct((512, 128), BF16),
        [pltpu.VMEM((512, 128), F32), *near],
        (False, False, False, far),
    )(perf, owner, slot, adj)


def owner_body(arrived, well, cross, *refs):
    out, sx, rq = refs[-3:]
    sx[...] = arrived[...].astype(F32)

    def rows(i):
        return jnp.concatenate(
            [sx[pl.ds(i, 64, stride=8), :], sx[pl.ds(i + 1, 64, stride=8), :]], axis=0
        )

    meta = rows(4)
    ident, row_code = meta[:, 0:1], meta[:, 1:2]
    panel = jnp.concatenate([rows(0), rows(2)], axis=1)
    i0, i1 = iota((SLOTS, SLOTS), 0), iota((SLOTS, SLOTS), 1)
    across = jnp.sum(jnp.where(i0 == i1, ident, 0.0), axis=0, keepdims=True)
    same = jnp.where(ident == across, 1.0, 0.0)
    totals = dot(same, panel).astype(BF16).astype(F32)
    mixed = jnp.zeros((SLOTS, 256), F32)
    for w in range(4):
        mine = ident == float(w + 1)
        mixed = mixed + dot(jnp.where(mine, panel, 0.0), well[w])
        mixed = mixed + dot(jnp.where(mine, totals, 0.0), cross[w])
    mixed = mixed.astype(BF16).astype(F32)
    tag = jnp.where(iota((SLOTS, 128), 1) == 96, row_code, 0.0)
    for k in range(2):
        part = slice(k * 64, (k + 1) * 64)
        for c in range(2):
            rq[pl.ds(2 * c + k, 64, stride=8), :] = mixed[part, c * 128 : (c + 1) * 128]
        rq[pl.ds(4 + k, 64, stride=8), :] = tag[part]
        rq[pl.ds(6 + k, 64, stride=8), :] = jnp.zeros((64, 128), F32)
    full = rq[...].reshape(64, 8, 128)
    sub, lane = iota((64, 8, 128), 1), iota((64, 8, 128), 2)

    def from_y(v, step):
        gap = jnp.zeros((8, 8, 128), F32)
        return jnp.concatenate([gap, v[:-8]] if step < 0 else [v[8:], gap], axis=0)

    def from_x(v, step):
        v = v.reshape(8, 8, 8, 128)
        gap = jnp.zeros((8, 1, 8, 128), F32)
        v = jnp.concatenate([gap, v[:, :-1]] if step < 0 else [v[:, 1:], gap], axis=1)
        return v.reshape(64, 8, 128)

    def turn(v, by):
        return pltpu.roll(v, by, 2)

    def half(v):
        return pltpu.roll(v, 4, 1)

    below, above = from_y(full, -1), from_y(full, 1)
    edge = jnp.where(lane >= 121, from_x(full, -1), jnp.where(lane < 7, from_x(full, 1), 0.0))
    edges = edge + turn(from_y(edge, -1), 32) + turn(from_y(edge, 1), 64)
    tags = jnp.where((sub >= 4) & (lane == 96), full, 0.0)
    tags = tags + turn(from_y(tags, -1), 1) + turn(from_y(tags, 1), 2)
    tags = tags + turn(from_x(tags, -1), 3) + turn(from_x(tags, 1), 6)
    first = jnp.where(sub < 4, full, half(below))
    second = jnp.where(sub < 4, above, half(jnp.where(sub < 4, edges, 0.0)) + tags)
    out[...] = jnp.concatenate([first, second], axis=1).astype(BF16)


def owner_work(arrived, well, cross, *after):
    return call(
        owner_body,
        jax.ShapeDtypeStruct((64, 16, 128), BF16),
        [pltpu.VMEM((512, 128), F32), pltpu.VMEM((512, 128), F32)],
        [False] * 3 + [True] * len(after),
    )(arrived, well, cross, *after)


def place_body(arrived, *refs):
    ins, (ws, wx, up, down, sx) = refs[:-5], refs[-5:]
    sx[...] = arrived[...].reshape(1024, 128).astype(F32)

    def rows(i):
        return jnp.concatenate(
            [sx[pl.ds(i, 64, stride=16), :], sx[pl.ds(i + 1, 64, stride=16), :]], axis=0
        )

    def both(i):
        return jnp.concatenate([rows(i), rows(i + 2)], axis=1)

    codes = rows(12).T

    def code(n):
        return codes[96 + n : 97 + n, :]

    def place(want, n, values):
        return dot(jnp.where(want == code(n), 1.0, 0.0), values)

    lane = jnp.bitwise_and(iota((SLOTS, 256), 1), 127)

    def sides(by):
        v = jnp.concatenate(
            [pltpu.roll(rows(12), by, 1) if by else rows(12), pltpu.roll(rows(14), by, 1) if by else rows(14)],
            axis=1,
        )
        return jnp.where(lane >= 121, v, 0.0), jnp.where(lane < 7, v, 0.0)

    own = (iota((256, SLOTS), 0) + 1).astype(F32)
    g = iota((64, SLOTS), 0)
    j = jnp.bitwise_and(g, 7)
    high = ((g - j) * 4 + j + 1).astype(F32)
    low = high + 24.0
    main = place(own, 0, both(0))
    above, below = place(high, 2, both(8)), place(low, 1, both(4))
    minus, plus = sides(0)
    side = place(own, 3, minus) + place(own, 6, plus)
    minus, plus = sides(96)
    side_below = place(low, 4, minus) + place(low, 7, plus)
    minus, plus = sides(64)
    side_above = place(high, 5, minus) + place(high, 8, plus)
    for c in range(2):
        part = slice(c * 128, (c + 1) * 128)

        def planes(v, v_above, v_below):
            v = v[:, part].reshape(8, 32, 128)
            v_above, v_below = (u[:, part].reshape(8, 8, 128) for u in (v_above, v_below))
            return [tall(v[z], v_above[z], v_below[z]) for z in range(NZ)]

        strip = jnp.zeros((EY, 128), F32)
        for z, plane in enumerate(planes(side, side_above, side_below)):
            strip = to_strip(plane, z, strip)
        wx[c] = strip
        mine = planes(main, above, below)
        for z in range(NZ):
            ws[c, z] = mine[z]
        first, strip = 4 if ins else 0, swap(strip)
        cols = ins[1][c] if ins else jnp.zeros((EY, 128), F32)
        for j in range(first):
            up[c, j] = ins[0][c, 4 + j].astype(BF16)
            down[c, j] = ins[0][c, j].astype(BF16)
        for j in range(3):
            up[c, first + j] = mine[5 + j].astype(BF16)
            down[c, first + j] = mine[j].astype(BF16)
        up[c, first + 3] = by_half(strip, cols).astype(BF16)
        down[c, first + 3] = by_half(cols, strip).astype(BF16)


def place(arrived, *ins):
    sent = jax.ShapeDtypeStruct((2, 8 if ins else 4, EY, 128), BF16)
    return call(
        place_body,
        (
            jax.ShapeDtypeStruct((2, NZ, EY, 128), F32),
            jax.ShapeDtypeStruct((2, EY, 128), F32),
            sent,
            sent,
        ),
        [pltpu.VMEM((1024, 128), F32)],
    )(arrived, *ins)


def fields_of(refs):
    adj, couple, diag, cross, source = refs
    out = [(adj, 0), (adj, 1)] + [(couple, i) for i in range(6)]
    return out + [(r, i) for r in (diag, cross, source) for i in range(2)]


def ysend_body(*refs):
    far, (up, down), near, sems = refs[:5], refs[6:8], refs[8:13], refs[13]
    pairs = [(a.at[:, :, 0:8], b.at[:, :, 0:8]) for a, b in zip(far, near)]
    pairs += [(a.at[:, :, 24:32], b.at[:, :, 8:16]) for a, b in zip(far, near)]
    for copy in start_copies(pairs, sems):
        copy.wait()
    for f, (ref, i) in enumerate(fields_of(near)):
        down[8 * f : 8 * f + 8] = ref[i, :, 0:8].astype(BF16)
        up[8 * f : 8 * f + 8] = ref[i, :, 8:16].astype(BF16)


def ysend(after, *ins):
    shape = jax.ShapeDtypeStruct((112, 8, 128), BF16)
    near = [pltpu.VMEM((a.shape[0], NZ, 16, NX), F32) for a in ins]
    near += [pltpu.SemaphoreType.DMA((2 * len(ins),))]
    return call(ysend_body, (shape, shape), near, [True] * 6)(*ins, after)


def block_planes(ref, i, f, ylo, yhi):
    return [
        tall(ref[i, z], yhi[8 * f + z].astype(F32), ylo[8 * f + z].astype(F32)) for z in range(NZ)
    ]


def xsend_body(*refs):
    ins, (ylo, yhi, _, out) = refs[:-4], refs[-4:]
    for f, (ref, i) in enumerate(fields_of(ins)):
        strip = jnp.zeros((EY, 128), F32)
        for z, plane in enumerate(block_planes(ref, i, f, ylo, yhi)):
            strip = to_strip(plane, z, strip)
        out[f] = strip.astype(BF16)


def xsend(after, *ins):
    shape = jax.ShapeDtypeStruct((14, EY, 128), BF16)
    return call(xsend_body, shape, far=[False] * len(ins) + [True])(*ins, after)


def z_slot(f):
    return (4 * f, 4) if f < 2 else (3 * f + 2, 3)


def zsend_body(*refs):
    ins, (ylo, yhi, xlo, xhi, _, up, down) = refs[:-7], refs[-7:]
    for f, (ref, i) in enumerate(fields_of(ins)):
        planes = block_planes(ref, i, f, ylo, yhi)
        at, deep = z_slot(f)
        for j in range(deep):
            up[at + j] = planes[NZ - deep + j].astype(BF16)
            down[at + j] = planes[j].astype(BF16)
    for q in range(7):
        even, odd = columns(xlo, xhi, 2 * q), swap(columns(xlo, xhi, 2 * q + 1))
        up[44 + q] = by_half(odd, even).astype(BF16)
        down[44 + q] = by_half(even, odd).astype(BF16)


def zsend(after, *ins):
    shape = jax.ShapeDtypeStruct((51, EY, NX), BF16)
    return call(zsend_body, (shape, shape), far=[False] * len(ins) + [True])(*ins, after)


def field_planes(ref, i, f, ylo, yhi, zlo, zhi):
    at, deep = z_slot(f)
    low = [zlo[at + j].astype(F32) for j in range(deep)]
    high = [zhi[at + j].astype(F32) for j in range(deep)]
    return low + block_planes(ref, i, f, ylo, yhi) + high


def field_strip(f, xlo, xhi, zlo, zhi):
    low, high = zlo[44 + f // 2].astype(F32), zhi[44 + f // 2].astype(F32)
    far = swap(by_half(low, high)) if f % 2 else by_half(high, low)
    return jnp.concatenate([columns(xlo, xhi, f), far], axis=1)


def half_group(z):
    return (0, z - 4) if 4 <= z < 12 else (1, (z - 12) % 16)


def sweeps_body(final, *refs):
    ins, ylo, yhi, xlo, xhi, zlo, zhi = refs[:5], *refs[5:11]
    field, fstrip, buf0, buf1, overs, rhs, rstrip = refs[-7:]
    if final:
        near, out = refs[11], refs[-8]
        ws, wx, wlo, whi = refs[12:16]
    else:
        out, out_strip = refs[-9:-7]
        ws, wx, wlo, whi = refs[11:15]
    bufs = (buf0, buf1)
    strips = []
    skip = 4 if final else 0
    lane = iota((EY, 128), 1)
    column = jnp.bitwise_and(iota((EY, 256), 1), 15)

    for c in range(2):
        if final:
            planes = [wlo[c, j].astype(F32) for j in range(4)]
            planes += [ins[0][c, z] for z in range(NZ)]
            planes += [whi[c, j].astype(F32) for j in range(4)]
        else:
            planes = field_planes(ins[0], c, c, ylo, yhi, zlo, zhi)
        for z, plane in enumerate(planes):
            buf0[c, z] = plane
        for e, plane in enumerate(field_planes(ins[4], c, 12 + c, ylo, yhi, zlo, zhi)):
            if e < 3:
                extra = wlo[c, skip + e].astype(F32)
            elif e >= 11:
                extra = whi[c, skip + e - 11].astype(F32)
            else:
                extra = ws[c, e - 3]
            rhs[c, e] = plane + extra
    for n, (ref, i) in enumerate(fields_of(ins)[2:12]):
        for e, plane in enumerate(field_planes(ref, i, n + 2, ylo, yhi, zlo, zhi)):
            field[n, e] = plane
        fstrip[n] = field_strip(n + 2, xlo, xhi, zlo, zhi)
    for c in range(2):
        low, high = wlo[c, skip + 3].astype(F32), whi[c, skip + 3].astype(F32)
        if final:
            strips.append(jnp.concatenate([near[c], by_half(high, low)], axis=1))
        else:
            strips.append(field_strip(c, xlo, xhi, zlo, zhi))
        side = jnp.concatenate([wx[c], swap(by_half(low, high))], axis=1)
        rstrip[c] = side + field_strip(12 + c, xlo, xhi, zlo, zhi)

    def mix(co, inflow):
        return co(6) * inflow[0] + co(8) * inflow[1], co(9) * inflow[0] + co(7) * inflow[1]

    for s in range(SWEEPS):
        last = s == SWEEPS - 1
        src, dst = bufs[s % 2], bufs[1 - s % 2]
        rows = NY if last and final else EY
        layers = range(1 + s, EZ - 1 - s)
        edges = []
        for c in range(2):
            edge = [jnp.zeros((EY, 128), F32)] * 2
            for z in layers:
                h, g = half_group(z)
                overs[c, z] = pltpu.roll(strips[c][:, 128 * h : 128 * h + 128], 120 - 16 * g, 1)
                if not (last and final):
                    edge[h] = to_strip(src[c, z], g, edge[h])
            edges.append(jnp.concatenate(edge, axis=1))

        for z in layers:

            def co(n):
                return field[n, z - 1, 0:rows]

            inflow = []
            for c in range(2):
                here, over = src[c, z], overs[c, z]
                right = pltpu.roll(jnp.where(lane == 0, over, here), 127, 1)
                left = pltpu.roll(jnp.where(lane == 127, over, here), 1, 1)
                total = rhs[c, z - 1, 0:rows]
                total = total + co(0) * src[c, z + 1, 0:rows]
                total = total + co(1) * src[c, z - 1, 0:rows]
                total = total + co(2) * pltpu.roll(here, EY - 1, 0)[0:rows]
                total = total + co(3) * pltpu.roll(here, 1, 0)[0:rows]
                total = total + co(4) * right[0:rows]
                total = total + co(5) * left[0:rows]
                inflow.append(total)
            for c, new in enumerate(mix(co, inflow)):
                if last:
                    out[c, z - 4] = new
                else:
                    dst[c, z] = new
        if last and final:
            break

        def co(n):
            return fstrip[n]

        inflow = []
        for c in range(2):
            here, edge = strips[c], edges[c]
            right = pltpu.roll(jnp.where(column == 8, edge, here), 255, 1)
            left = pltpu.roll(jnp.where(column == 7, edge, here), 1, 1)
            total = rstrip[c]
            total = total + co(0) * pltpu.roll(here, 240, 1) + co(1) * pltpu.roll(here, 16, 1)
            total = total + co(2) * pltpu.roll(here, EY - 1, 0) + co(3) * pltpu.roll(here, 1, 0)
            total = total + co(4) * right + co(5) * left
            inflow.append(total)
        strips = list(mix(co, inflow))
    if not final:
        for c in range(2):
            out_strip[c] = strips[c][:, 0:128]


def sweeps(final, *ins):
    shape = jax.ShapeDtypeStruct((2, NZ, NY if final else EY, NX), F32)
    return call(
        functools.partial(sweeps_body, final),
        shape if final else (shape, jax.ShapeDtypeStruct((2, EY, 128), F32)),
        [
            pltpu.VMEM((10, CZ, EY, 128), F32),
            pltpu.VMEM((10, EY, 256), F32),
            pltpu.VMEM((2, EZ, EY, 128), F32),
            pltpu.VMEM((2, EZ, EY, 128), F32),
            pltpu.VMEM((2, EZ, EY, 128), F32),
            pltpu.VMEM((2, CZ, EY, 128), F32),
            pltpu.VMEM((2, EY, 256), F32),
        ],
    )(*ins)


def exchange(up, down, axis):
    count = lax.axis_size(axis)
    forward = [(i, i + 1) for i in range(count - 1)]
    backward = [(i + 1, i) for i in range(count - 1)]
    return lax.ppermute(up, axis, forward), lax.ppermute(down, axis, backward)


def per_device(
    source,
    adjoint_start,
    couple,
    diag_inverse,
    cross_inverse,
    perf_row,
    well_owner,
    well_slot,
    well_block,
    cross_block,
):
    perf = perf_row.reshape(1, -1)
    owner = well_owner.reshape(1, -1)
    slot = well_slot.reshape(1, -1)
    well = well_block.reshape(well_block.shape[3:])
    cross_mats = cross_block.reshape(cross_block.shape[3:])
    fields = (couple, diag_inverse, cross_inverse, source)
    start = (adjoint_start, *fields)
    sent = panels(adjoint_start, perf, owner, slot, far=True)
    arrived = lax.all_to_all(sent, ("gy", "gx"), split_axis=0, concat_axis=0, tiled=True)
    ylo, yhi = exchange(*ysend(sent, *start), "gy")
    answers = owner_work(arrived, well, cross_mats)
    answers, ylo, yhi = lax.optimization_barrier((answers, ylo, yhi))
    packed = xsend(answers, *start, ylo, yhi)
    halo = (ylo, yhi, *exchange(packed, packed, "gx"))
    returned = lax.all_to_all(answers, ("gy", "gx"), split_axis=0, concat_axis=0, tiled=True)
    kept = (*fields, *halo, *exchange(*zsend(returned, *start, *halo), "gz"))
    ws, wx, up, down = place(returned)
    adjoint, strip = sweeps(False, *start[:1], *kept, ws, wx, *exchange(up, down, "gz"))

    sent = panels(adjoint, perf, owner, slot)
    arrived = lax.all_to_all(sent, ("gy", "gx"), split_axis=0, concat_axis=0, tiled=True)
    answers = owner_work(arrived, well, cross_mats)
    returned = lax.all_to_all(answers, ("gy", "gx"), split_axis=0, concat_axis=0, tiled=True)
    ws, wx, up, down = place(returned, adjoint, strip)
    return sweeps(True, adjoint, *kept, strip, ws, wx, *exchange(up, down, "gz"))


def solution(mesh):
    placed = (
        P(None, "gz", "gy", "gx"),
        P(None, "gz", "gy", "gx"),
        P(None, "gz", "gy", "gx"),
        P(None, "gz", "gy", "gx"),
        P(None, "gz", "gy", "gx"),
        P("gz", "gy", "gx", None),
        P("gz", "gy", "gx", None, None),
        P("gz", "gy", "gx", None),
        P("gz", "gy", "gx", None, None, None),
        P("gz", "gy", "gx", None, None, None),
    )
    return jax.shard_map(
        per_device, mesh=mesh, in_specs=placed, out_specs=P(None, "gz", "gy", "gx"), check_vma=False
    )
```

```python
import functools

import jax
import jax.numpy as jnp
from jax import lax
from jax.experimental import pallas as pl
from jax.experimental.pallas import tpu as pltpu
from jax.sharding import PartitionSpec as P

SWEEPS = 4
F32 = jnp.float32
BF16 = jnp.bfloat16
NZ, NY, NX = 8, 32, 128
EZ, EY = 16, 48
OWNERS = 64
SLOTS = 128
CZ = 14


def iota(shape, dim):
    return lax.broadcasted_iota(jnp.int32, shape, dim)


def call(body, out_shape, scratch=(), far=None):
    specs, limit = {}, 32
    if far is not None:
        limit = 58 if all(far) else 32
        specs["in_specs"] = [pl.BlockSpec(memory_space=pl.ANY if f else pltpu.VMEM) for f in far]
    return pl.pallas_call(
        body,
        out_shape=out_shape,
        scratch_shapes=list(scratch),
        compiler_params=pltpu.CompilerParams(vmem_limit_bytes=limit * 1024 * 1024),
        **specs,
    )


def start_copies(pairs, sems):
    copies = [pltpu.make_async_copy(a, b, sems.at[i]) for i, (a, b) in enumerate(pairs)]
    for copy in copies:
        copy.start()
    return copies


def dot(a, b):
    return jnp.dot(a.astype(BF16), b.astype(BF16), preferred_element_type=F32)


def lane_group():
    return lax.shift_right_logical(iota((EY, 128), 1), 4)


def first_eight():
    return jnp.bitwise_and(iota((EY, 128), 1), 15) < 8


def columns(xlo, xhi, index):
    below, above = xlo[index // 2].astype(F32), xhi[index // 2].astype(F32)
    if index % 2:
        below, above = pltpu.roll(below, 120, 1), pltpu.roll(above, 8, 1)
    return jnp.where(first_eight(), below, above)


def to_strip(plane, g, strip):
    return jnp.where(lane_group() == g, pltpu.roll(plane, 16 * g + 8, 1), strip)


def swap(strip):
    return pltpu.roll(strip, 64, 1)


def by_half(low, high):
    return jnp.where(lane_group() < 4, low, high)


def tall(main, above, below):
    return jnp.concatenate([main, above, below], axis=0)


def panels_body(perf, owner, slot, adj, out, sc, *near):
    far = len(near) > 0
    if far:
        near, sems = near
        (copy,) = start_copies([(adj, near)], sems)
    own = owner[...].astype(F32)
    i0, i1 = iota((64, 64), 0), iota((64, 64), 1)
    wide = jnp.broadcast_to(own, (64, 64))
    down = jnp.sum(jnp.where(i0 == i1, wide, 0.0), axis=1, keepdims=True)
    rank = jnp.sum(jnp.where((down == wide) & (i0 < i1), 1.0, 0.0), axis=0, keepdims=True)
    dest = rank * float(OWNERS) + own
    hit = iota((SLOTS, 64), 0).astype(F32) == dest
    row_code = jnp.sum(jnp.where(hit, perf[...].astype(F32) + 1.0, 0.0), axis=1, keepdims=True)
    slot_code = jnp.sum(jnp.where(hit, slot[...].astype(F32) + 1.0, 0.0), axis=1, keepdims=True)
    pick = jnp.where(row_code == (iota((SLOTS, 256), 1) + 1).astype(F32), 1.0, 0.0)
    lane = iota((SLOTS, 128), 1)
    meta = jnp.where(lane == 0, slot_code, jnp.where(lane == 1, row_code, 0.0))
    if far:
        copy.wait()
        adj = near
    for c in range(2):
        picked = dot(pick, adj[c, :, 0:NY].reshape(NZ * NY, NX))
        for k in range(2):
            sc[pl.ds(2 * c + k, 64, stride=8), :] = picked[k * 64 : (k + 1) * 64]
    zero = jnp.zeros((64, 128), F32)
    for k in range(2):
        sc[pl.ds(4 + k, 64, stride=8), :] = meta[k * 64 : (k + 1) * 64]
        sc[pl.ds(6 + k, 64, stride=8), :] = zero
    out[...] = sc[...].astype(BF16)


def panels(adj, perf, owner, slot, far=False):
    near = [pltpu.VMEM(adj.shape, F32), pltpu.SemaphoreType.DMA((1,))] if far else []
    return call(
        panels_body,
        jax.ShapeDtypeStruct((512, 128), BF16),
        [pltpu.VMEM((512, 128), F32), *near],
        (False, False, False, far),
    )(perf, owner, slot, adj)


def owner_body(arrived, well, cross, *refs):
    out, sx, rq = refs[-3:]
    sx[...] = arrived[...].astype(F32)

    def rows(i):
        return jnp.concatenate(
            [sx[pl.ds(i, 64, stride=8), :], sx[pl.ds(i + 1, 64, stride=8), :]], axis=0
        )

    meta = rows(4)
    ident, row_code = meta[:, 0:1], meta[:, 1:2]
    panel = jnp.concatenate([rows(0), rows(2)], axis=1)
    i0, i1 = iota((SLOTS, SLOTS), 0), iota((SLOTS, SLOTS), 1)
    across = jnp.sum(jnp.where(i0 == i1, ident, 0.0), axis=0, keepdims=True)
    same = jnp.where(ident == across, 1.0, 0.0)
    totals = dot(same, panel).astype(BF16).astype(F32)
    mixed = jnp.zeros((SLOTS, 256), F32)
    for w in range(4):
        mine = ident == float(w + 1)
        mixed = mixed + dot(jnp.where(mine, panel, 0.0), well[w])
        mixed = mixed + dot(jnp.where(mine, totals, 0.0), cross[w])
    mixed = mixed.astype(BF16).astype(F32)
    tag = jnp.where(iota((SLOTS, 128), 1) == 96, row_code, 0.0)
    for k in range(2):
        part = slice(k * 64, (k + 1) * 64)
        for c in range(2):
            rq[pl.ds(2 * c + k, 64, stride=8), :] = mixed[part, c * 128 : (c + 1) * 128]
        rq[pl.ds(4 + k, 64, stride=8), :] = tag[part]
        rq[pl.ds(6 + k, 64, stride=8), :] = jnp.zeros((64, 128), F32)
    full = rq[...].reshape(64, 8, 128)
    sub, lane = iota((64, 8, 128), 1), iota((64, 8, 128), 2)

    def from_y(v, step):
        gap = jnp.zeros((8, 8, 128), F32)
        return jnp.concatenate([gap, v[:-8]] if step < 0 else [v[8:], gap], axis=0)

    def from_x(v, step):
        v = v.reshape(8, 8, 8, 128)
        gap = jnp.zeros((8, 1, 8, 128), F32)
        v = jnp.concatenate([gap, v[:, :-1]] if step < 0 else [v[:, 1:], gap], axis=1)
        return v.reshape(64, 8, 128)

    def turn(v, by):
        return pltpu.roll(v, by, 2)

    def half(v):
        return pltpu.roll(v, 4, 1)

    below, above = from_y(full, -1), from_y(full, 1)
    edge = jnp.where(lane >= 121, from_x(full, -1), jnp.where(lane < 7, from_x(full, 1), 0.0))
    edges = edge + turn(from_y(edge, -1), 32) + turn(from_y(edge, 1), 64)
    tags = jnp.where((sub >= 4) & (lane == 96), full, 0.0)
    tags = tags + turn(from_y(tags, -1), 1) + turn(from_y(tags, 1), 2)
    tags = tags + turn(from_x(tags, -1), 3) + turn(from_x(tags, 1), 6)
    first = jnp.where(sub < 4, full, half(below))
    second = jnp.where(sub < 4, above, half(jnp.where(sub < 4, edges, 0.0)) + tags)
    out[...] = jnp.concatenate([first, second], axis=1).astype(BF16)


def owner_work(arrived, well, cross, *after):
    return call(
        owner_body,
        jax.ShapeDtypeStruct((64, 16, 128), BF16),
        [pltpu.VMEM((512, 128), F32), pltpu.VMEM((512, 128), F32)],
        [False] * 3 + [True] * len(after),
    )(arrived, well, cross, *after)


def place_body(arrived, *refs):
    ins, (ws, wx, up, down, sx) = refs[:-5], refs[-5:]
    sx[...] = arrived[...].reshape(1024, 128).astype(F32)

    def rows(i):
        return jnp.concatenate(
            [sx[pl.ds(i, 64, stride=16), :], sx[pl.ds(i + 1, 64, stride=16), :]], axis=0
        )

    def both(i):
        return jnp.concatenate([rows(i), rows(i + 2)], axis=1)

    codes = rows(12).T

    def code(n):
        return codes[96 + n : 97 + n, :]

    def place(want, n, values):
        return dot(jnp.where(want == code(n), 1.0, 0.0), values)

    lane = jnp.bitwise_and(iota((SLOTS, 256), 1), 127)

    def sides(by):
        v = jnp.concatenate(
            [pltpu.roll(rows(12), by, 1) if by else rows(12), pltpu.roll(rows(14), by, 1) if by else rows(14)],
            axis=1,
        )
        return jnp.where(lane >= 121, v, 0.0), jnp.where(lane < 7, v, 0.0)

    own = (iota((256, SLOTS), 0) + 1).astype(F32)
    g = iota((64, SLOTS), 0)
    j = jnp.bitwise_and(g, 7)
    high = ((g - j) * 4 + j + 1).astype(F32)
    low = high + 24.0
    main = place(own, 0, both(0))
    above, below = place(high, 2, both(8)), place(low, 1, both(4))
    minus, plus = sides(0)
    side = place(own, 3, minus) + place(own, 6, plus)
    minus, plus = sides(96)
    side_below = place(low, 4, minus) + place(low, 7, plus)
    minus, plus = sides(64)
    side_above = place(high, 5, minus) + place(high, 8, plus)
    for c in range(2):
        part = slice(c * 128, (c + 1) * 128)

        def planes(v, v_above, v_below):
            v = v[:, part].reshape(8, 32, 128)
            v_above, v_below = (u[:, part].reshape(8, 8, 128) for u in (v_above, v_below))
            return [tall(v[z], v_above[z], v_below[z]) for z in range(NZ)]

        strip = jnp.zeros((EY, 128), F32)
        for z, plane in enumerate(planes(side, side_above, side_below)):
            strip = to_strip(plane, z, strip)
        wx[c] = strip
        mine = planes(main, above, below)
        for z in range(NZ):
            ws[c, z] = mine[z]
        first, strip = 4 if ins else 0, swap(strip)
        cols = ins[1][c] if ins else jnp.zeros((EY, 128), F32)
        for j in range(first):
            up[c, j] = ins[0][c, 4 + j].astype(BF16)
            down[c, j] = ins[0][c, j].astype(BF16)
        for j in range(3):
            up[c, first + j] = mine[5 + j].astype(BF16)
            down[c, first + j] = mine[j].astype(BF16)
        up[c, first + 3] = by_half(strip, cols).astype(BF16)
        down[c, first + 3] = by_half(cols, strip).astype(BF16)


def place(arrived, *ins):
    sent = jax.ShapeDtypeStruct((2, 8 if ins else 4, EY, 128), BF16)
    return call(
        place_body,
        (
            jax.ShapeDtypeStruct((2, NZ, EY, 128), F32),
            jax.ShapeDtypeStruct((2, EY, 128), F32),
            sent,
            sent,
        ),
        [pltpu.VMEM((1024, 128), F32)],
    )(arrived, *ins)


def fields_of(refs):
    adj, couple, diag, cross, source = refs
    out = [(adj, 0), (adj, 1)] + [(couple, i) for i in range(6)]
    return out + [(r, i) for r in (diag, cross, source) for i in range(2)]


def ysend_body(*refs):
    far, (up, down), near, sems = refs[:5], refs[6:8], refs[8:13], refs[13]
    pairs = [(a.at[:, :, 0:8], b.at[:, :, 0:8]) for a, b in zip(far, near)]
    pairs += [(a.at[:, :, 24:32], b.at[:, :, 8:16]) for a, b in zip(far, near)]
    for copy in start_copies(pairs, sems):
        copy.wait()
    for f, (ref, i) in enumerate(fields_of(near)):
        down[8 * f : 8 * f + 8] = ref[i, :, 0:8].astype(BF16)
        up[8 * f : 8 * f + 8] = ref[i, :, 8:16].astype(BF16)


def ysend(after, *ins):
    shape = jax.ShapeDtypeStruct((112, 8, 128), BF16)
    near = [pltpu.VMEM((a.shape[0], NZ, 16, NX), F32) for a in ins]
    near += [pltpu.SemaphoreType.DMA((2 * len(ins),))]
    return call(ysend_body, (shape, shape), near, [True] * 6)(*ins, after)


def block_planes(ref, i, f, ylo, yhi):
    return [
        tall(ref[i, z], yhi[8 * f + z].astype(F32), ylo[8 * f + z].astype(F32)) for z in range(NZ)
    ]


def xsend_body(*refs):
    ins, (ylo, yhi, _, up, down) = refs[:-5], refs[-5:]
    strips = []
    for f, (ref, i) in enumerate(fields_of(ins)):
        strip = jnp.zeros((EY, 128), F32)
        for z, plane in enumerate(block_planes(ref, i, f, ylo, yhi)):
            strip = to_strip(plane, z, strip)
        strips.append(strip)
        if f % 2:
            even, odd = strips[f - 1], strip
            up[f // 2] = jnp.where(first_eight(), even, pltpu.roll(odd, 8, 1)).astype(BF16)
            down[f // 2] = jnp.where(first_eight(), pltpu.roll(odd, 120, 1), even).astype(BF16)


def xsend(after, *ins):
    shape = jax.ShapeDtypeStruct((7, EY, 128), BF16)
    return call(xsend_body, (shape, shape), far=[False] * len(ins) + [True])(*ins, after)


def z_slot(f):
    return (4 * f, 4) if f < 2 else (3 * f + 2, 3)


def zsend_body(*refs):
    ins, (ylo, yhi, xlo, xhi, _, up, down) = refs[:-7], refs[-7:]
    for f, (ref, i) in enumerate(fields_of(ins)):
        planes = block_planes(ref, i, f, ylo, yhi)
        at, deep = z_slot(f)
        for j in range(deep):
            up[at + j] = planes[NZ - deep + j].astype(BF16)
            down[at + j] = planes[j].astype(BF16)
    for q in range(7):
        even, odd = columns(xlo, xhi, 2 * q), swap(columns(xlo, xhi, 2 * q + 1))
        up[44 + q] = by_half(odd, even).astype(BF16)
        down[44 + q] = by_half(even, odd).astype(BF16)


def zsend(after, *ins):
    shape = jax.ShapeDtypeStruct((51, EY, NX), BF16)
    return call(zsend_body, (shape, shape), far=[False] * len(ins) + [True])(*ins, after)


def field_planes(ref, i, f, ylo, yhi, zlo, zhi):
    at, deep = z_slot(f)
    low = [zlo[at + j].astype(F32) for j in range(deep)]
    high = [zhi[at + j].astype(F32) for j in range(deep)]
    return low + block_planes(ref, i, f, ylo, yhi) + high


def field_strip(f, xlo, xhi, zlo, zhi):
    low, high = zlo[44 + f // 2].astype(F32), zhi[44 + f // 2].astype(F32)
    far = swap(by_half(low, high)) if f % 2 else by_half(high, low)
    return jnp.concatenate([columns(xlo, xhi, f), far], axis=1)


def half_group(z):
    return (0, z - 4) if 4 <= z < 12 else (1, (z - 12) % 16)


def sweeps_body(final, *refs):
    ins, ylo, yhi, xlo, xhi, zlo, zhi = refs[:5], *refs[5:11]
    field, fstrip, buf0, buf1, overs, rhs, rstrip = refs[-7:]
    if final:
        near, out = refs[11], refs[-8]
        ws, wx, wlo, whi = refs[12:16]
    else:
        out, out_strip = refs[-9:-7]
        ws, wx, wlo, whi = refs[11:15]
    bufs = (buf0, buf1)
    strips = []
    skip = 4 if final else 0
    lane = iota((EY, 128), 1)
    column = jnp.bitwise_and(iota((EY, 256), 1), 15)

    for c in range(2):
        if final:
            planes = [wlo[c, j].astype(F32) for j in range(4)]
            planes += [ins[0][c, z] for z in range(NZ)]
            planes += [whi[c, j].astype(F32) for j in range(4)]
        else:
            planes = field_planes(ins[0], c, c, ylo, yhi, zlo, zhi)
        for z, plane in enumerate(planes):
            buf0[c, z] = plane
        for e, plane in enumerate(field_planes(ins[4], c, 12 + c, ylo, yhi, zlo, zhi)):
            if e < 3:
                extra = wlo[c, skip + e].astype(F32)
            elif e >= 11:
                extra = whi[c, skip + e - 11].astype(F32)
            else:
                extra = ws[c, e - 3]
            rhs[c, e] = plane + extra
    for n, (ref, i) in enumerate(fields_of(ins)[2:12]):
        for e, plane in enumerate(field_planes(ref, i, n + 2, ylo, yhi, zlo, zhi)):
            field[n, e] = plane
        fstrip[n] = field_strip(n + 2, xlo, xhi, zlo, zhi)
    for c in range(2):
        low, high = wlo[c, skip + 3].astype(F32), whi[c, skip + 3].astype(F32)
        if final:
            strips.append(jnp.concatenate([near[c], by_half(high, low)], axis=1))
        else:
            strips.append(field_strip(c, xlo, xhi, zlo, zhi))
        side = jnp.concatenate([wx[c], swap(by_half(low, high))], axis=1)
        rstrip[c] = side + field_strip(12 + c, xlo, xhi, zlo, zhi)

    def mix(co, inflow):
        return co(6) * inflow[0] + co(8) * inflow[1], co(9) * inflow[0] + co(7) * inflow[1]

    for s in range(SWEEPS):
        last = s == SWEEPS - 1
        src, dst = bufs[s % 2], bufs[1 - s % 2]
        rows = NY if last and final else EY
        layers = range(1 + s, EZ - 1 - s)
        edges = []
        for c in range(2):
            edge = [jnp.zeros((EY, 128), F32)] * 2
            for z in layers:
                h, g = half_group(z)
                overs[c, z] = pltpu.roll(strips[c][:, 128 * h : 128 * h + 128], 120 - 16 * g, 1)
                if not (last and final):
                    edge[h] = to_strip(src[c, z], g, edge[h])
            edges.append(jnp.concatenate(edge, axis=1))

        for z in layers:

            def co(n):
                return field[n, z - 1, 0:rows]

            inflow = []
            for c in range(2):
                here, over = src[c, z], overs[c, z]
                right = pltpu.roll(jnp.where(lane == 0, over, here), 127, 1)
                left = pltpu.roll(jnp.where(lane == 127, over, here), 1, 1)
                total = rhs[c, z - 1, 0:rows]
                total = total + co(0) * src[c, z + 1, 0:rows]
                total = total + co(1) * src[c, z - 1, 0:rows]
                total = total + co(2) * pltpu.roll(here, EY - 1, 0)[0:rows]
                total = total + co(3) * pltpu.roll(here, 1, 0)[0:rows]
                total = total + co(4) * right[0:rows]
                total = total + co(5) * left[0:rows]
                inflow.append(total)
            for c, new in enumerate(mix(co, inflow)):
                if last:
                    out[c, z - 4] = new
                else:
                    dst[c, z] = new
        if last and final:
            break

        def co(n):
            return fstrip[n]

        inflow = []
        for c in range(2):
            here, edge = strips[c], edges[c]
            right = pltpu.roll(jnp.where(column == 8, edge, here), 255, 1)
            left = pltpu.roll(jnp.where(column == 7, edge, here), 1, 1)
            total = rstrip[c]
            total = total + co(0) * pltpu.roll(here, 240, 1) + co(1) * pltpu.roll(here, 16, 1)
            total = total + co(2) * pltpu.roll(here, EY - 1, 0) + co(3) * pltpu.roll(here, 1, 0)
            total = total + co(4) * right + co(5) * left
            inflow.append(total)
        strips = list(mix(co, inflow))
    if not final:
        for c in range(2):
            out_strip[c] = strips[c][:, 0:128]


def sweeps(final, *ins):
    shape = jax.ShapeDtypeStruct((2, NZ, NY if final else EY, NX), F32)
    return call(
        functools.partial(sweeps_body, final),
        shape if final else (shape, jax.ShapeDtypeStruct((2, EY, 128), F32)),
        [
            pltpu.VMEM((10, CZ, EY, 128), F32),
            pltpu.VMEM((10, EY, 256), F32),
            pltpu.VMEM((2, EZ, EY, 128), F32),
            pltpu.VMEM((2, EZ, EY, 128), F32),
            pltpu.VMEM((2, EZ, EY, 128), F32),
            pltpu.VMEM((2, CZ, EY, 128), F32),
            pltpu.VMEM((2, EY, 256), F32),
        ],
    )(*ins)


def exchange(up, down, axis):
    count = lax.axis_size(axis)
    forward = [(i, i + 1) for i in range(count - 1)]
    backward = [(i + 1, i) for i in range(count - 1)]
    return lax.ppermute(up, axis, forward), lax.ppermute(down, axis, backward)


def per_device(
    source,
    adjoint_start,
    couple,
    diag_inverse,
    cross_inverse,
    perf_row,
    well_owner,
    well_slot,
    well_block,
    cross_block,
):
    perf = perf_row.reshape(1, -1)
    owner = well_owner.reshape(1, -1)
    slot = well_slot.reshape(1, -1)
    well = well_block.reshape(well_block.shape[3:])
    cross_mats = cross_block.reshape(cross_block.shape[3:])
    fields = (couple, diag_inverse, cross_inverse, source)
    start = (adjoint_start, *fields)
    sent = panels(adjoint_start, perf, owner, slot, far=True)
    arrived = lax.all_to_all(sent, ("gy", "gx"), split_axis=0, concat_axis=0, tiled=True)
    ylo, yhi = exchange(*ysend(sent, *start), "gy")
    answers = owner_work(arrived, well, cross_mats)
    answers, ylo, yhi = lax.optimization_barrier((answers, ylo, yhi))
    halo = (ylo, yhi, *exchange(*xsend(answers, *start, ylo, yhi), "gx"))
    returned = lax.all_to_all(answers, ("gy", "gx"), split_axis=0, concat_axis=0, tiled=True)
    kept = (*fields, *halo, *exchange(*zsend(returned, *start, *halo), "gz"))
    ws, wx, up, down = place(returned)
    adjoint, strip = sweeps(False, *start[:1], *kept, ws, wx, *exchange(up, down, "gz"))

    sent = panels(adjoint, perf, owner, slot)
    arrived = lax.all_to_all(sent, ("gy", "gx"), split_axis=0, concat_axis=0, tiled=True)
    answers = owner_work(arrived, well, cross_mats)
    returned = lax.all_to_all(answers, ("gy", "gx"), split_axis=0, concat_axis=0, tiled=True)
    ws, wx, up, down = place(returned, adjoint, strip)
    return sweeps(True, adjoint, *kept, strip, ws, wx, *exchange(up, down, "gz"))


def solution(mesh):
    placed = (
        P(None, "gz", "gy", "gx"),
        P(None, "gz", "gy", "gx"),
        P(None, "gz", "gy", "gx"),
        P(None, "gz", "gy", "gx"),
        P(None, "gz", "gy", "gx"),
        P("gz", "gy", "gx", None),
        P("gz", "gy", "gx", None, None),
        P("gz", "gy", "gx", None),
        P("gz", "gy", "gx", None, None, None),
        P("gz", "gy", "gx", None, None, None),
    )
    return jax.shard_map(
        per_device, mesh=mesh, in_specs=placed, out_specs=P(None, "gz", "gy", "gx"), check_vma=False
    )
```
